32 devices in a mesh: dp: 2 (over x), row: 4 (over z), col: 4 (over y, core).
Axes of the slice: x: 2, y: 2, z: 4, core: 2. Of those that a mesh axis runs over, the one named last changes fastest.
Arguments:
- block_in: float32 [2048, 1152], P(('dp', 'col'), 'row'), may hold values from -6 to 6
- labels: int32 [2], P('dp'), may hold values from 0 to 1000
- steps_t: int32 [2], P('dp'), may hold values from 0 to 999
- out_cot: float32 [2048, 1152], P(('dp', 'col'), 'row'), may hold values from -6 to 6
- class_table: float32 [1001, 1152], P(None, 'col'), may hold values from -6 to 6
- w_ada: float32 [1152, 6, 1152], P('col', None, 'row'), may hold values from -0.1875 to 0.1875
- b_ada: float32 [6, 1152], P(None, 'row'), may hold values from -3 to 3
- w_qkv: float32 [1152, 3, 1152], P('row', None, 'col'), may hold values from -0.125 to 0.125
- b_qv: float32 [2, 1152], P(None, 'col'), may hold values from -3 to 3
- w_out: float32 [1152, 1152], P('col', 'row'), may hold values from -3.5 to 3.5
- b_out: float32 [1152], P('row'), may hold values from -3 to 3
- w_up: float32 [1152, 4608], P('row', 'col'), may hold values from -0.1875 to 0.1875
- b_up: float32 [4608], P('col'), may hold values from -3 to 3
- w_down: float32 [4608, 1152], P('col', 'row'), may hold values from -0.09375 to 0.09375
- b_down: float32 [1152], P('row'), may hold values from -3 to 3
Outputs:
- block_out: float32 [2048, 1152], P(('dp', 'col'), 'row')
- in_grad: float32 [2048, 1152], P(('dp', 'col'), 'row')
- table_grad: float32 [1001, 1152], P(None, 'col')
- ada_grad: float32 [1152, 6, 1152], P('col', None, 'row')
- ada_bias_grad: float32 [6, 1152], P(None, 'row')
- qkv_grad: float32 [1152, 3, 1152], P('row', None, 'col')
- qv_bias_grad: float32 [2, 1152], P(None, 'col')
- out_grad: float32 [1152, 1152], P('col', 'row')
- out_bias_grad: float32 [1152], P('row')
- up_grad: float32 [1152, 4608], P('row', 'col')
- up_bias_grad: float32 [4608], P('col')
- down_grad: float32 [4608, 1152], P('col', 'row')
- down_bias_grad: float32 [1152], P('row')
The draws below stay inside these ranges and needn't reach their ends.
All inputs are finite; a program needn't handle non-finite values.
Results may differ from the reference program's by a relative error of at most 0.0003.
Values sent between devices are 32-bit elements; how exact they have to be, the bound alone decides.
No kernel may reach another device: no remote copies, remote signals or barrier semaphores. Data moves between devices by JAX's collectives and lax.ppermute only.
A program may use at most 128 MiB of HBM per device.

```python
import math
import jax
import jax.numpy as jnp
from jax import lax

D = 1152
HEADS = 16
HD = 72
FF = 4608
CLASSES = 1001
SEQ = 1024
TIMESTEPS = 1000
LATENTS = 2
TOKENS = 2048


def level_of(own_key, shape, cuts, low, largest):
    loudness = 1.0
    for dim, blocks in cuts:
        heights = jax.random.uniform(jax.random.fold_in(jax.random.fold_in(own_key, 6), dim), (blocks,), jnp.float32, low / len(cuts), largest / len(cuts))
        loudness = loudness * jnp.repeat(jnp.exp(heights), shape[dim] // blocks).reshape((-1,) + (1,) * (len(shape) - 1 - dim))
    return loudness


def scatter_about(rng, shape, scale, most, pieces=(), dtype=jnp.bfloat16):
    entries = jax.random.normal(rng, shape, jnp.float32) * scale
    if len(pieces) > 0:
        entries = level_of(rng, shape, pieces, -0.22, 0.18) * entries
    return jnp.clip(entries, min=-most, max=most).astype(dtype)


def setup_inputs(seed: int = 0) -> dict:
    seeds = jax.random.split(jax.random.key(seed), 16)
    return {
        "block_in": scatter_about(seeds[0], (TOKENS, D), 1.0, 6.0, ((0, 8), (1, 4)), jnp.float32),
        "labels": jax.random.randint(seeds[1], (LATENTS,), 0, CLASSES).astype(jnp.int32),
        "steps_t": jax.random.randint(seeds[2], (LATENTS,), 0, TIMESTEPS).astype(jnp.int32),
        "out_cot": scatter_about(seeds[3], (TOKENS, D), 1.0, 6.0, ((0, 8), (1, 4)), jnp.float32),
        "class_table": scatter_about(seeds[4], (CLASSES, D), 1.0, 6.0, ((1, 4),), jnp.float32),
        "w_ada": scatter_about(seeds[5], (D, 6, D), D ** -0.5, 0.1875, ((0, 4), (2, 4)), jnp.float32),
        "b_ada": scatter_about(seeds[6], (6, D), 0.5, 3.0, ((1, 4),), jnp.float32),
        "w_qkv": scatter_about(seeds[7], (D, 3, D), (2 * D) ** -0.5, 0.125, ((0, 4), (2, 4)), jnp.float32),
        "b_qv": scatter_about(seeds[8], (2, D), 0.5, 3.0, ((1, 4),), jnp.float32),
        "w_out": scatter_about(seeds[9], (D, D), (max(D // 384, 1)) ** -0.5, 3.5, ((0, 4), (1, 4)), jnp.float32),
        "b_out": scatter_about(seeds[10], (D,), 0.5, 3.0, ((0, 4),), jnp.float32),
        "w_up": scatter_about(seeds[11], (D, FF), D ** -0.5, 0.1875, ((0, 4), (1, 4)), jnp.float32),
        "b_up": scatter_about(seeds[12], (FF,), 0.5, 3.0, ((0, 4),), jnp.float32),
        "w_down": scatter_about(seeds[13], (FF, D), FF ** -0.5, 0.09375, ((0, 4), (1, 4)), jnp.float32),
        "b_down": scatter_about(seeds[14], (D,), 0.5, 3.0, ((0, 4),), jnp.float32),
    }


exact_mode = lax.Precision.HIGHEST
norm_epsilon = 1e-06

def matmul(left, right):
    return jnp.dot(left, right, precision=exact_mode, preferred_element_type=jnp.float32)

def normalize(values):
    center = lax.optimization_barrier(jnp.mean(values, axis=-1, keepdims=True))
    centred = values - center
    spread = lax.optimization_barrier(jnp.mean(centred * centred, axis=-1, keepdims=True))
    return centred * lax.rsqrt(spread + norm_epsilon)

def time_features(steps_t):
    half_width = D // 2
    frequency = jnp.exp(-math.log(10000.0) * jnp.arange(half_width).astype(jnp.float32) / half_width)
    angles = steps_t.astype(jnp.float32)[:, None] * frequency[None, :]
    return jnp.concatenate([jnp.cos(angles), jnp.sin(angles)], axis=1)

def block_forward(tokens, cond_row, w_ada, b_ada, w_qkv, b_qv, w_out, b_out, w_up, b_up, w_down, b_down):
    modulation = matmul(jax.nn.silu(cond_row)[None, :], w_ada.reshape(D, 6 * D)).reshape(6, D) + b_ada
    normed_one = normalize(tokens)
    hidden_one = normed_one * (1.0 + modulation[1]) + modulation[0]
    qkv_values = matmul(hidden_one, w_qkv.reshape(D, 3 * D)).reshape(SEQ, 3, D)
    queries = (qkv_values[:, 0] + b_qv[0]).reshape(SEQ, HEADS, HD)
    keys_all = qkv_values[:, 1].reshape(SEQ, HEADS, HD)
    values_all = (qkv_values[:, 2] + b_qv[1]).reshape(SEQ, HEADS, HD)
    scores = jnp.einsum('qhd,khd->hqk', queries, keys_all, precision=exact_mode) * (1.0 / math.sqrt(HD))
    weights = jnp.exp(scores)
    row_sums = lax.optimization_barrier(jnp.sum(weights, axis=2, keepdims=True))
    attended = jnp.einsum('hqk,khd->qhd', weights / row_sums, values_all, precision=exact_mode).reshape(SEQ, D)
    attn_out = matmul(attended, w_out) + b_out
    mixed = tokens + modulation[2] * attn_out
    normed_two = normalize(mixed)
    hidden_two = normed_two * (1.0 + modulation[4]) + modulation[3]
    activated = jax.nn.gelu(matmul(hidden_two, w_up) + b_up, approximate=True)
    return mixed + modulation[5] * (matmul(activated, w_down) + b_down)

def reference(block_in, labels, steps_t, out_cot, class_table, w_ada, b_ada, w_qkv, b_qv, w_out, b_out, w_up, b_up, w_down, b_down):
    conditions = class_table[labels] + time_features(steps_t)
    params = (w_ada, b_ada, w_qkv, b_qv, w_out, b_out, w_up, b_up, w_down, b_down)
    tokens = block_in.reshape(LATENTS, SEQ, D)
    cotangents = out_cot.reshape(LATENTS, SEQ, D)

    def per_latent(totals, scan_item):
        latent_tokens, cond_row, latent_cot = scan_item
        result, pullback = jax.vjp(block_forward, latent_tokens, cond_row, *params)
        grads = pullback(latent_cot)
        summed = tuple((left + right for left, right in zip(totals, grads[2:])))
        return (summed, (result, grads[0], grads[1]))
    start_totals = tuple((jnp.zeros_like(param) for param in params))
    totals, (outputs, in_grads, cond_grads) = lax.scan(per_latent, start_totals, (tokens, conditions, cotangents))
    table_grad = jnp.zeros_like(class_table).at[labels].add(cond_grads)
    return (outputs.reshape(TOKENS, D), in_grads.reshape(TOKENS, D), table_grad, totals[0], totals[1], totals[2], totals[3], totals[4], totals[5], totals[6], totals[7], totals[8], totals[9])
```

```python
import math

import jax
import jax.numpy as jnp
from jax import lax
from jax.sharding import PartitionSpec as P

HD = 72
norm_epsilon = 1e-06
fast_mode = lax.Precision.HIGH
exact_mode = lax.Precision.HIGHEST


def contract(left, right, left_dim, right_dim, precision=fast_mode):
    return lax.dot_general(
        left,
        right,
        (((left_dim,), (right_dim,)), ((), ())),
        precision=precision,
        preferred_element_type=jnp.float32,
    )


def gather_all(local):
    return lax.all_gather(local, ("col", "row"), axis=0, tiled=True)


def scatter_all(partial):
    return lax.psum_scatter(partial, ("col", "row"), scatter_dimension=0, tiled=True)


def row_swap(blocks):
    count = lax.axis_size("row")
    me = lax.axis_index("row")
    result = jnp.zeros_like(blocks)
    own = lax.dynamic_index_in_dim(blocks, me, 0, keepdims=True)
    result = lax.dynamic_update_slice_in_dim(result, own, me, 0)
    for step in range(1, count):
        outgoing = lax.dynamic_index_in_dim(blocks, (me + step) % count, 0, keepdims=True)
        incoming = lax.ppermute(
            outgoing, "row", [(i, (i + step) % count) for i in range(count)]
        )
        result = lax.dynamic_update_slice_in_dim(result, incoming, (me - step) % count, 0)
    return result


def to_tokens(local):
    count = lax.axis_size("row")
    rows, width = local.shape
    blocks = row_swap(local.reshape(count, rows // count, width))
    return blocks.transpose(1, 0, 2).reshape(rows // count, count * width)


def from_tokens(local):
    count = lax.axis_size("row")
    rows, width = local.shape
    blocks = row_swap(local.reshape(rows, count, width // count).transpose(1, 0, 2))
    return blocks.reshape(rows * count, width // count)


def dp_total(local):
    if lax.axis_size("dp") == 2:
        return local + lax.ppermute(local, "dp", [(0, 1), (1, 0)])
    return lax.psum(local, "dp")


def normalize(values):
    center = jnp.mean(values, axis=1, keepdims=True)
    centred = values - center
    spread = jnp.mean(centred * centred, axis=1, keepdims=True)
    inverse = lax.rsqrt(spread + norm_epsilon)
    return (centred * inverse, inverse)


def normalize_back(grad_values, normed, inverse):
    totals = jnp.mean(grad_values, axis=1, keepdims=True)
    along = jnp.mean(grad_values * normed, axis=1, keepdims=True)
    return inverse * (grad_values - totals - normed * along)


def shards(
    block_in,
    labels,
    steps_t,
    out_cot,
    class_table,
    w_ada,
    b_ada,
    w_qkv,
    b_qv,
    w_out,
    b_out,
    w_up,
    b_up,
    w_down,
    b_down,
):
    rows = lax.axis_size("row")
    cols = lax.axis_size("col")
    me_row = lax.axis_index("row")
    me_col = lax.axis_index("col")
    tok_local, width_row = block_in.shape
    width = width_row * rows
    tokens = tok_local * cols
    tok_own = tok_local // rows
    width_col = w_out.shape[0]
    heads_col = width_col // HD
    heads_own = max(1, heads_col // rows)
    copies = max(1, rows // heads_col)
    head_width = heads_own * HD
    head_groups = rows // copies
    hidden_own = w_up.shape[1] // rows
    own_token = (me_col * rows + me_row) * tok_own

    in_own = to_tokens(block_in)
    in_all = gather_all(in_own)
    qkv_blocks = (
        w_qkv.reshape(width_row, 3, head_groups, head_width)
        .transpose(2, 0, 1, 3)
        .reshape(head_groups, width_row, 3 * head_width)
    )
    qkv_matrix = row_swap(jnp.repeat(qkv_blocks, copies, axis=0)).reshape(width, 3 * head_width)
    cot_own = to_tokens(out_cot)
    cot_all = gather_all(cot_own)
    out_blocks = w_out.reshape(rows, width_col // rows, width_row)
    out_rows = row_swap(out_blocks).transpose(1, 0, 2).reshape(width_col // rows, width)
    out_matrix = gather_all(out_rows)
    up_matrix = row_swap(
        w_up.reshape(width_row, rows, hidden_own).transpose(1, 0, 2)
    ).reshape(width, hidden_own)
    down_matrix = (
        row_swap(w_down.reshape(rows, hidden_own, width_row))
        .transpose(1, 0, 2)
        .reshape(hidden_own, width)
    )

    feature = me_col * width_col + jnp.arange(width_col)
    half_width = width // 2
    frequency = jnp.exp(
        -math.log(10000.0) * (feature % half_width).astype(jnp.float32) / half_width
    )
    angles = steps_t.astype(jnp.float32)[:, None] * frequency[None, :]
    own_class = lax.dynamic_slice_in_dim(class_table, labels[0], 1, 0)
    condition = own_class + jnp.where(
        feature[None, :] < half_width, jnp.cos(angles), jnp.sin(angles)
    )
    silu_cond, silu_pull = jax.vjp(jax.nn.silu, condition)
    ada_terms = contract(silu_cond, w_ada.reshape(width_col, 6 * width_row), 1, 0, exact_mode)
    small = jnp.concatenate(
        [ada_terms.reshape(6, width_row), b_ada, b_out[None], b_down[None]], axis=0
    )
    small_all = lax.all_gather(small, ("col", "row"), axis=0, tiled=False)
    small_all = small_all.reshape(cols, rows, small.shape[0], width_row)
    modulation = jnp.sum(small_all[:, :, :6], axis=0) + small_all[0, :, 6:12]
    modulation = modulation.transpose(1, 0, 2).reshape(6, 1, width)
    shift_one, scale_one, gate_one, shift_two, scale_two, gate_two = modulation
    out_bias = small_all[0, :, 12].reshape(1, width)
    down_bias = small_all[0, :, 13].reshape(1, width)

    normed_one, _ = normalize(in_all)
    hidden_one = normed_one * (1.0 + scale_one) + shift_one
    head_start = (me_row // copies) * head_width
    head_bias = lax.dynamic_slice_in_dim(b_qv, head_start, head_width, 1)
    qkv = contract(hidden_one, qkv_matrix, 1, 0).reshape(tokens, 3, heads_own, HD)
    queries = qkv[:, 0] + head_bias[0].reshape(heads_own, HD)
    keys = qkv[:, 1]
    values = qkv[:, 2] + head_bias[1].reshape(heads_own, HD)
    factor = 1.0 / math.sqrt(HD)
    scores = jnp.einsum("qhd,khd->hqk", queries, keys, precision=fast_mode) * factor
    weights = jnp.exp(scores)
    weights = weights / jnp.sum(weights, axis=2, keepdims=True)
    attended_own = jnp.einsum("hqk,khd->hdq", weights, values, precision=fast_mode)
    attended_flip = gather_all(attended_own.reshape(head_width, tokens))
    if copies > 1:
        attended_flip = (
            attended_flip.reshape(cols, head_groups, copies, head_width, tokens)[:, :, 0]
        ).reshape(width, tokens)

    attn_out = contract(attended_flip, out_matrix, 0, 0) + out_bias
    mixed = in_all + gate_one * attn_out
    normed_two, inverse_two = normalize(mixed)
    hidden_two = normed_two * (1.0 + scale_two) + shift_two
    up_bias = lax.dynamic_slice_in_dim(b_up, me_row * hidden_own, hidden_own, 0)
    up_values = contract(hidden_two, up_matrix, 1, 0) + up_bias
    activated, gelu_pull = jax.vjp(lambda u: jax.nn.gelu(u, approximate=True), up_values)
    d_mlp = cot_all * gate_two
    d_activated = contract(d_mlp, down_matrix, 1, 1)
    (d_up,) = gelu_pull(d_activated)
    d_hidden_two = gather_all(scatter_all(contract(d_up, up_matrix, 1, 1)))
    mlp_own = scatter_all(contract(activated, down_matrix, 1, 0)) + down_bias
    mixed_own = lax.dynamic_slice_in_dim(mixed, own_token, tok_own, 0)
    block_out = from_tokens(mixed_own + gate_two * mlp_own)
    up_grad = contract(hidden_two, d_up, 0, 0)
    down_grad = contract(activated, d_mlp, 0, 0)
    up_bias_grad = jnp.sum(d_up, axis=0)
    down_bias_grad = jnp.sum(d_mlp, axis=0)

    d_mixed = cot_all + normalize_back(d_hidden_two * (1.0 + scale_two), normed_two, inverse_two)
    d_attn = d_mixed * gate_one
    d_attended = contract(d_attn, out_rows_for_heads(out_rows, out_matrix, copies, head_width), 1, 1)
    d_attended = d_attended.reshape(tokens, heads_own, HD)
    attended_col = lax.dynamic_slice_in_dim(attended_flip, me_col * width_col, width_col, 0)
    d_attn_row = lax.dynamic_slice_in_dim(d_attn, me_row * width_row, width_row, 1)
    out_grad = contract(attended_col, d_attn_row, 1, 0)
    out_bias_grad = jnp.sum(d_attn, axis=0)

    d_weights = jnp.einsum("qhd,khd->hqk", d_attended, values, precision=fast_mode)
    row_dots = jnp.sum(weights * d_weights, axis=2, keepdims=True)
    d_scores = weights * (d_weights - row_dots) * factor
    d_query = jnp.einsum("hqk,khd->qhd", d_scores, keys, precision=fast_mode)
    d_key = jnp.einsum("hqk,qhd->khd", d_scores, queries, precision=fast_mode)
    d_value = jnp.einsum("hqk,qhd->khd", weights, d_attended, precision=fast_mode)
    d_qkv = jnp.stack([d_query, d_key, d_value], axis=1).reshape(tokens, 3 * head_width)
    d_hidden_one = scatter_all(contract(d_qkv, qkv_matrix, 1, 1) * (1.0 / copies))
    qkv_grad = contract(hidden_one, d_qkv, 0, 0)
    d_qkv_sums = jnp.sum(d_qkv, axis=0).reshape(3, head_width)

    normed_own, inverse_own = normalize(in_own)
    d_mixed_own = lax.dynamic_slice_in_dim(d_mixed, own_token, tok_own, 0)
    in_grad = from_tokens(
        d_mixed_own + normalize_back(d_hidden_one * (1.0 + scale_one), normed_own, inverse_own)
    )

    up_grad = row_swap(up_grad.reshape(rows, width_row, hidden_own))
    up_grad = up_grad.transpose(1, 0, 2).reshape(width_row, rows * hidden_own)
    down_grad = row_swap(down_grad.reshape(hidden_own, rows, width_row).transpose(1, 0, 2))
    down_grad = down_grad.reshape(rows * hidden_own, width_row)
    qkv_grad = row_swap(qkv_grad.reshape(rows, width_row, 3 * head_width))[::copies]
    qkv_grad = qkv_grad.reshape(head_groups, width_row, 3, head_width).transpose(1, 2, 0, 3)
    qkv_grad = qkv_grad.reshape(width_row, 3, width_col)
    bias_all = lax.all_gather(
        jnp.concatenate([up_bias_grad, d_qkv_sums[0], d_qkv_sums[2]]), "row", axis=0, tiled=False
    )
    up_bias_grad = bias_all[:, :hidden_own].reshape(-1)
    qv_bias_grad = bias_all[::copies, hidden_own:].reshape(head_groups, 2, head_width)
    qv_bias_grad = qv_bias_grad.transpose(1, 0, 2).reshape(2, width_col)
    out_bias_grad = lax.dynamic_slice_in_dim(out_bias_grad, me_row * width_row, width_row, 0)
    down_bias_grad = lax.dynamic_slice_in_dim(down_bias_grad, me_row * width_row, width_row, 0)

    own_sums = jnp.stack(
        [
            jnp.sum(d_hidden_one, axis=0),
            jnp.sum(d_hidden_one * normed_own, axis=0),
            jnp.sum(cot_own * mlp_own, axis=0),
        ]
    )
    own_sums = lax.psum(own_sums, ("row", "col"))
    mod_grads = jnp.stack(
        [
            own_sums[0],
            own_sums[1],
            jnp.sum(d_mixed * attn_out, axis=0),
            jnp.sum(d_hidden_two, axis=0),
            jnp.sum(d_hidden_two * normed_two, axis=0),
            own_sums[2],
        ]
    )
    mod_grads = lax.dynamic_slice_in_dim(mod_grads, me_row * width_row, width_row, 1)
    silu_grads = lax.psum(
        contract(
            mod_grads.reshape(1, 6 * width_row),
            w_ada.reshape(width_col, 6 * width_row),
            1,
            1,
            exact_mode,
        ),
        "row",
    )
    (cond_grad,) = silu_pull(silu_grads)
    cond_pack = jnp.concatenate(
        [silu_cond, cond_grad, mod_grads.reshape(1, 6 * width_row)], axis=1
    )
    cond_all = lax.all_gather(cond_pack, "dp", axis=0, tiled=True)
    label_all = lax.all_gather(labels.astype(jnp.float32), "dp", axis=0, tiled=True)
    silu_all = cond_all[:, :width_col]
    mod_all = cond_all[:, 2 * width_col :]
    label_hot = (
        label_all[:, None].astype(jnp.int32) == jnp.arange(class_table.shape[0])[None, :]
    ).astype(jnp.float32)
    table_grad = contract(label_hot, cond_all[:, width_col : 2 * width_col], 0, 0, exact_mode)
    ada_grad = contract(silu_all, mod_all, 0, 0, exact_mode).reshape(width_col, 6, width_row)
    ada_bias_grad = jnp.sum(mod_all, axis=0).reshape(6, width_row)
    return (
        block_out,
        in_grad,
        table_grad,
        ada_grad,
        ada_bias_grad,
        dp_total(qkv_grad),
        dp_total(qv_bias_grad),
        dp_total(out_grad),
        dp_total(out_bias_grad),
        dp_total(up_grad),
        dp_total(up_bias_grad),
        dp_total(down_grad),
        dp_total(down_bias_grad),
    )


def out_rows_for_heads(out_rows, out_matrix, copies, head_width):
    if copies == 1:
        return out_rows
    start = (lax.axis_index("col") * (lax.axis_size("row") // copies)) * head_width
    start = start + (lax.axis_index("row") // copies) * head_width
    return lax.dynamic_slice_in_dim(out_matrix, start, head_width, 0)


def solution(mesh):
    in_specs = (
        P(("dp", "col"), "row"),
        P("dp"),
        P("dp"),
        P(("dp", "col"), "row"),
        P(None, "col"),
        P("col", None, "row"),
        P(None, "row"),
        P("row", None, "col"),
        P(None, "col"),
        P("col", "row"),
        P("row"),
        P("row", "col"),
        P("col"),
        P("col", "row"),
        P("row"),
    )
    out_specs = (
        P(("dp", "col"), "row"),
        P(("dp", "col"), "row"),
        P(None, "col"),
        P("col", None, "row"),
        P(None, "row"),
        P("row", None, "col"),
        P(None, "col"),
        P("col", "row"),
        P("row"),
        P("row", "col"),
        P("col"),
        P("col", "row"),
        P("row"),
    )
    return jax.shard_map(shards, mesh=mesh, in_specs=in_specs, out_specs=out_specs, check_vma=False)
```

```python
from functools import partial
import math

import jax
import jax.numpy as jnp
from jax import lax
from jax.experimental.layout import Layout, with_layout_constraint
from jax.sharding import PartitionSpec as P

HD = 72
norm_epsilon = 1e-06
fast_mode = lax.Precision.HIGH
exact_mode = lax.Precision.HIGHEST


def contract(left, right, left_dim, right_dim, precision=fast_mode):
    return lax.dot_general(
        left,
        right,
        (((left_dim,), (right_dim,)), ((), ())),
        precision=precision,
        preferred_element_type=jnp.float32,
    )


def row_major(values):
    return with_layout_constraint(values, Layout(major_to_minor=tuple(range(values.ndim))))


def shift_row(values, step):
    count = lax.axis_size("row")
    if step % count == 0:
        return values
    return lax.ppermute(values, "row", [(i, (i + step) % count) for i in range(count)])


def shift_chip(values, step):
    count = lax.axis_size("col") // 2
    if step % count == 0:
        return values
    pairs = [
        (2 * i + core, 2 * ((i + step) % count) + core) for i in range(count) for core in range(2)
    ]
    return lax.ppermute(values, "col", pairs)


def swap_core(values):
    return lax.ppermute(values, "col", [(i, i ^ 1) for i in range(lax.axis_size("col"))])


def swap_dp(values):
    return lax.ppermute(values, "dp", [(0, 1), (1, 0)])


def butterfly(values, axis):
    count = lax.axis_size(axis)
    step = 1
    while step < count:
        values = values + lax.ppermute(values, axis, [(i, i ^ step) for i in range(count)])
        step *= 2
    return values


def row_order():
    count = lax.axis_size("row")
    return sorted(range(count), key=lambda step: (min(step, count - step), step))


def spread(block):
    count = lax.axis_size("row")
    chips = lax.axis_size("col") // 2
    by_step = {0: block}
    for step in row_order()[1:]:
        if step <= count // 2:
            by_step[step] = shift_row(by_step[step - 1], 1)
        else:
            by_step[step] = shift_row(by_step[(step + 1) % count], -1)
    groups = []
    for step in row_order():
        groups.append([shift_chip(by_step[step], chip) for chip in range(chips)])
    near = jnp.concatenate(sum(groups[:-1], []), axis=0)
    far = jnp.concatenate(groups[-1], axis=0)
    return [near, far, swap_core(near), swap_core(far)]


def gather_tokens(block):
    return jnp.concatenate(spread(block), axis=0)


def scatter_tokens(partial_sums):
    count = lax.axis_size("row")
    chips = lax.axis_size("col") // 2
    half = partial_sums.shape[0] // 2
    group = half // count
    size = group // chips
    split = half - group
    far = partial_sums[split:half] + swap_core(partial_sums[half + split :])
    near = partial_sums[:split] + swap_core(partial_sums[half : half + split])
    sums = {}
    for place, step in reversed(list(enumerate(row_order()))):
        part = far if place == count - 1 else near[place * group : (place + 1) * group]
        total = part[:size]
        for chip in range(1, chips):
            total = total + shift_chip(part[chip * size : (chip + 1) * size], -chip)
        sums[step] = total
    for step in reversed(row_order()[1:]):
        if step <= count // 2:
            sums[step - 1] = sums[step - 1] + shift_row(sums[step], -1)
        else:
            back = (step + 1) % count
            sums[back] = sums[back] + shift_row(sums[step], 1)
    return sums[0]


def heads_to_tokens(values):
    count = lax.axis_size("row")
    chips = lax.axis_size("col") // 2
    half = values.shape[0] // 2
    values = jnp.concatenate([values[:half], swap_core(values[half:])], axis=1)
    order = row_order()
    group = half // count
    parts = []
    for step in order:
        place = order.index(-step % count)
        parts.append(shift_row(values[place * group : (place + 1) * group], step))
    values = jnp.concatenate(parts, axis=1)
    size = group // chips
    parts = []
    for step in range(chips):
        place = -step % chips
        parts.append(shift_chip(values[place * size : (place + 1) * size], step))
    return jnp.concatenate(parts, axis=1)


def tokens_to_heads(values):
    count = lax.axis_size("row")
    chips = lax.axis_size("col") // 2
    order = row_order()
    size = values.shape[1] // chips
    parts = []
    for step in range(chips):
        place = -step % chips
        parts.append(shift_chip(values[:, place * size : (place + 1) * size], step))
    values = jnp.concatenate(parts, axis=0)
    group = size // count
    parts = []
    for step in order:
        place = order.index(-step % count)
        parts.append(shift_row(values[:, place * group : (place + 1) * group], step))
    values = jnp.concatenate(parts, axis=0)
    half = group // 2
    return jnp.concatenate([values[:, :half], swap_core(values[:, half:])], axis=0)


def head_order(pieces):
    count = lax.axis_size("row")
    chips = lax.axis_size("col") // 2
    cores = [jnp.concatenate(pieces[:2], axis=0), jnp.concatenate(pieces[2:], axis=0)]
    size = cores[0].shape[0] // (count * chips)
    parts = []
    for chip in range(chips):
        for place in range(count):
            for core in range(2):
                start = (place * chips + chip) * size
                parts.append(cores[core][start : start + size])
    return jnp.concatenate(parts, axis=0)


def row_parts(blocks):
    count = lax.axis_size("row")
    me = lax.axis_index("row")
    return [
        shift_row(lax.dynamic_index_in_dim(blocks, (me + step) % count, 0, keepdims=False), step)
        for step in range(count)
    ]


def by_source(parts):
    count = lax.axis_size("row")
    me = lax.axis_index("row")
    stacked = jnp.stack(parts)
    return [
        lax.dynamic_index_in_dim(stacked, (me - row) % count, 0, keepdims=False)
        for row in range(count)
    ]


def to_tokens(local):
    count = lax.axis_size("row")
    rows, width = local.shape
    return jnp.concatenate(by_source(row_parts(local.reshape(count, rows // count, width))), axis=1)


def from_tokens(local):
    count = lax.axis_size("row")
    width = local.shape[1] // count
    blocks = jnp.stack([local[:, i * width : (i + 1) * width] for i in range(count)])
    return jnp.concatenate(by_source(row_parts(blocks)), axis=0)


def fetch_weight(blocks):
    count, rows, width = blocks.shape
    blocks = row_major(blocks)
    if lax.axis_size("dp") != 2:
        return jnp.concatenate(by_source(row_parts(blocks)), axis=0)
    me = lax.axis_index("dp")
    half = rows // 2
    mine = jnp.stack(row_parts(lax.dynamic_slice_in_dim(blocks, me * half, half, 1)))
    mine = row_major(mine)
    both = jnp.stack([mine, swap_dp(mine)])
    low = by_source(list(lax.dynamic_index_in_dim(both, me, 0, keepdims=False)))
    high = by_source(list(lax.dynamic_index_in_dim(both, 1 - me, 0, keepdims=False)))
    return jnp.concatenate([part for pair in zip(low, high) for part in pair], axis=0)


def return_grad(grad):
    count = lax.axis_size("row")
    rows, width = grad.shape[0] // count, grad.shape[1]
    if lax.axis_size("dp") != 2:
        parts = by_source(row_parts(row_major(grad.reshape(count, rows, width))))
        return [lax.psum(part, "dp") for part in parts]
    me = lax.axis_index("dp")
    half = rows // 2
    halves = row_major(grad.reshape(count, 2, half, width))
    given = lax.dynamic_index_in_dim(halves, 1 - me, 1, keepdims=False)
    kept = lax.dynamic_index_in_dim(halves, me, 1, keepdims=False)
    mine = row_major(jnp.stack(row_parts(row_major(kept + swap_dp(given)))))
    both = jnp.stack([mine, swap_dp(mine)])
    low = by_source(list(lax.dynamic_index_in_dim(both, me, 0, keepdims=False)))
    high = by_source(list(lax.dynamic_index_in_dim(both, 1 - me, 0, keepdims=False)))
    return [jnp.concatenate(pair, axis=0) for pair in zip(low, high)]


def dp_stack(values):
    if lax.axis_size("dp") == 2:
        both = jnp.stack([values, swap_dp(values)])
        me = lax.axis_index("dp")
        return jnp.stack(
            [
                lax.dynamic_index_in_dim(both, me, 0, keepdims=False),
                lax.dynamic_index_in_dim(both, 1 - me, 0, keepdims=False),
            ]
        )
    return lax.all_gather(values, "dp", axis=0, tiled=False)


def normalize(values):
    center = jnp.mean(values, axis=1, keepdims=True)
    centred = values - center
    spread_of = jnp.mean(centred * centred, axis=1, keepdims=True)
    inverse = lax.rsqrt(spread_of + norm_epsilon)
    return (centred * inverse, inverse)


def normalize_back(grad_values, normed, inverse):
    totals = jnp.mean(grad_values, axis=1, keepdims=True)
    along = jnp.mean(grad_values * normed, axis=1, keepdims=True)
    return inverse * (grad_values - totals - normed * along)


def shards(
    block_in,
    labels,
    steps_t,
    out_cot,
    class_table,
    w_ada,
    b_ada,
    w_qkv,
    b_qv,
    w_out,
    b_out,
    w_up,
    b_up,
    w_down,
    b_down,
):
    rows = lax.axis_size("row")
    me_row = lax.axis_index("row")
    me_col = lax.axis_index("col")
    tok_local, width_row = block_in.shape
    width = width_row * rows
    width_col = w_out.shape[0]
    heads_col = width_col // HD
    heads_own = max(1, heads_col // rows)
    copies = max(1, rows // heads_col)
    head_width = heads_own * HD
    head_groups = rows // copies
    hidden_own = w_up.shape[1] // rows

    feature = me_col * width_col + jnp.arange(width_col)
    half_width = width // 2
    frequency = jnp.exp(
        -math.log(10000.0) * (feature % half_width).astype(jnp.float32) / half_width
    )
    angles = steps_t.astype(jnp.float32)[:, None] * frequency[None, :]
    own_class = lax.dynamic_slice_in_dim(class_table, labels[0], 1, 0)
    condition = own_class + jnp.where(
        feature[None, :] < half_width, jnp.cos(angles), jnp.sin(angles)
    )
    silu_cond, silu_pull = jax.vjp(jax.nn.silu, condition)
    ada_flat = w_ada.reshape(width_col, 6 * width_row)
    ada_terms = contract(silu_cond, ada_flat, 1, 0, exact_mode).reshape(6, width_row)
    ada_terms = butterfly(ada_terms, "col") + b_ada
    small = jnp.concatenate([ada_terms, b_out[None], b_down[None]], axis=0)
    small = by_source([shift_row(small, step) for step in range(rows)])
    small = jnp.concatenate(small, axis=1)[:, None, :]
    shift_one, scale_one, gate_one, shift_two, scale_two, gate_two, out_bias, down_bias = small

    in_own = to_tokens(block_in)
    normed_one, inverse_one = normalize(in_own)
    hidden_one = gather_tokens(normed_one * (1.0 + scale_one) + shift_one)
    tokens = hidden_one.shape[0]
    qkv_blocks = (
        w_qkv.reshape(width_row, 3, head_groups, head_width)
        .transpose(2, 0, 1, 3)
        .reshape(head_groups, width_row, 3 * head_width)
    )
    qkv_matrix = fetch_weight(jnp.repeat(qkv_blocks, copies, axis=0))
    head_start = (me_row // copies) * head_width
    head_bias = lax.dynamic_slice_in_dim(b_qv, head_start, head_width, 1)
    qkv = contract(hidden_one, qkv_matrix, 1, 0).reshape(tokens, 3, heads_own, HD)
    queries = qkv[:, 0] + head_bias[0].reshape(heads_own, HD)
    keys = qkv[:, 1]
    values = qkv[:, 2] + head_bias[1].reshape(heads_own, HD)
    factor = 1.0 / math.sqrt(HD)
    scores = jnp.einsum("qhd,khd->hqk", queries, keys, precision=fast_mode) * factor
    weights = jnp.exp(scores)
    weights = weights / jnp.sum(weights, axis=2, keepdims=True)
    attended = jnp.einsum("hqk,khd->qhd", weights, values, precision=fast_mode)
    attended = attended.reshape(tokens, head_width)
    if copies > 1:
        attended = jnp.where(me_row % copies == 0, attended, 0.0)
    attended_own = heads_to_tokens(attended)

    out_blocks = jnp.repeat(w_out.reshape(head_groups, head_width, width_row), copies, axis=0)
    out_rows = jnp.concatenate(by_source(row_parts(out_blocks)), axis=1)
    out_matrix = head_order(spread(out_rows))
    attn_out = contract(attended_own, out_matrix, 1, 0) + out_bias
    mixed = in_own + gate_one * attn_out
    normed_two, inverse_two = normalize(mixed)
    hidden_two = gather_tokens(normed_two * (1.0 + scale_two) + shift_two)

    cot_own = to_tokens(out_cot)
    d_mlp_own = cot_own * gate_two
    d_mlp = gather_tokens(d_mlp_own)
    up_matrix = fetch_weight(
        jnp.stack([w_up[:, i * hidden_own : (i + 1) * hidden_own] for i in range(rows)])
    )
    down_matrix = fetch_weight(
        w_down.reshape(rows, hidden_own, width_row).transpose(0, 2, 1)
    )
    up_bias = lax.dynamic_slice_in_dim(b_up, me_row * hidden_own, hidden_own, 0)
    up_values = contract(hidden_two, up_matrix, 1, 0) + up_bias
    activated, gelu_pull = jax.vjp(partial(jax.nn.gelu, approximate=True), up_values)
    d_activated = contract(d_mlp, down_matrix, 1, 0)
    (d_up,) = gelu_pull(d_activated)
    d_hidden_two = scatter_tokens(contract(d_up, up_matrix, 1, 1))
    mlp_own = scatter_tokens(contract(activated, down_matrix, 1, 1)) + down_bias
    block_out = from_tokens(mixed + gate_two * mlp_own)
    up_grad = jnp.concatenate(return_grad(contract(hidden_two, d_up, 0, 0)), axis=1)
    down_grad = jnp.concatenate(return_grad(contract(d_mlp, activated, 0, 0)), axis=1).T

    d_mixed = cot_own + normalize_back(d_hidden_two * (1.0 + scale_two), normed_two, inverse_two)
    d_attn_own = d_mixed * gate_one
    d_attended = tokens_to_heads(contract(d_attn_own, out_matrix, 1, 1))
    d_attended = d_attended.reshape(tokens, heads_own, HD)
    d_weights = jnp.einsum("qhd,khd->hqk", d_attended, values, precision=fast_mode)
    row_dots = jnp.sum(weights * d_weights, axis=2, keepdims=True)
    d_scores = weights * (d_weights - row_dots) * factor
    d_query = jnp.einsum("hqk,khd->qhd", d_scores, keys, precision=fast_mode)
    d_key = jnp.einsum("hqk,qhd->khd", d_scores, queries, precision=fast_mode)
    d_value = jnp.einsum("hqk,qhd->khd", weights, d_attended, precision=fast_mode)
    d_qkv = jnp.stack([d_query, d_key, d_value], axis=1).reshape(tokens, 3 * head_width)
    d_hidden_one = scatter_tokens(contract(d_qkv, qkv_matrix, 1, 1) * (1.0 / copies))
    in_grad = from_tokens(
        d_mixed + normalize_back(d_hidden_one * (1.0 + scale_one), normed_one, inverse_one)
    )
    qkv_grad = return_grad(contract(hidden_one, d_qkv, 0, 0))[::copies]
    qkv_grad = jnp.stack([part.reshape(width_row, 3, head_width) for part in qkv_grad], axis=2)
    qkv_grad = qkv_grad.reshape(width_row, 3, width_col)
    d_attn = gather_tokens(d_attn_own)
    out_grad = contract(attended, d_attn, 0, 0)
    out_grad = jnp.stack([out_grad[:, i * width_row : (i + 1) * width_row] for i in range(rows)])
    out_grad = jnp.concatenate(by_source(row_parts(out_grad))[::copies], axis=0)
    out_grad = jnp.sum(dp_stack(out_grad), axis=0)

    unit_sums = jnp.concatenate([jnp.sum(d_up, axis=0), jnp.sum(d_qkv, axis=0)])
    unit_sums = jnp.stack(by_source([shift_row(unit_sums, step) for step in range(rows)]))
    unit_sums = jnp.sum(dp_stack(unit_sums), axis=0)
    up_bias_grad = unit_sums[:, :hidden_own].reshape(-1)
    qkv_sums = unit_sums[::copies, hidden_own:].reshape(head_groups, 3, head_width)
    qv_bias_grad = jnp.stack([qkv_sums[:, 0].reshape(-1), qkv_sums[:, 2].reshape(-1)])
    own_sums = jnp.stack(
        [
            jnp.sum(d_hidden_one, axis=0),
            jnp.sum(d_hidden_one * normed_one, axis=0),
            jnp.sum(d_mixed * attn_out, axis=0),
            jnp.sum(d_hidden_two, axis=0),
            jnp.sum(d_hidden_two * normed_two, axis=0),
            jnp.sum(cot_own * mlp_own, axis=0),
            jnp.sum(d_attn_own, axis=0),
            jnp.sum(d_mlp_own, axis=0),
        ]
    )
    own_sums = butterfly(butterfly(own_sums, "col"), "row")
    own_sums = lax.dynamic_slice_in_dim(own_sums, me_row * width_row, width_row, 1)
    mod_grads = own_sums[:6].reshape(1, 6 * width_row)
    silu_grads = butterfly(contract(mod_grads, ada_flat, 1, 1, exact_mode), "row")
    (cond_grad,) = silu_pull(silu_grads)
    label_row = jnp.broadcast_to(labels.astype(jnp.float32)[:, None], (1, 128))
    pack = jnp.concatenate(
        [silu_cond, cond_grad, own_sums.reshape(1, 8 * width_row), label_row], axis=1
    )
    pack = dp_stack(pack[0])
    silu_all = pack[:, :width_col]
    cond_all = pack[:, width_col : 2 * width_col]
    sums_all = pack[:, 2 * width_col : 2 * width_col + 8 * width_row]
    label_all = pack[:, -1].astype(jnp.int32)
    label_hot = (label_all[:, None] == jnp.arange(class_table.shape[0])[None, :]).astype(
        jnp.float32
    )
    table_grad = contract(label_hot, cond_all, 0, 0, exact_mode)
    ada_grad = contract(silu_all, sums_all[:, : 6 * width_row], 0, 0, exact_mode)
    bias_sums = jnp.sum(sums_all, axis=0).reshape(8, width_row)
    return (
        block_out,
        in_grad,
        table_grad,
        ada_grad.reshape(width_col, 6, width_row),
        bias_sums[:6],
        qkv_grad,
        qv_bias_grad,
        out_grad,
        bias_sums[6],
        up_grad,
        up_bias_grad,
        down_grad,
        bias_sums[7],
    )


def solution(mesh):
    in_specs = (
        P(("dp", "col"), "row"),
        P("dp"),
        P("dp"),
        P(("dp", "col"), "row"),
        P(None, "col"),
        P("col", None, "row"),
        P(None, "row"),
        P("row", None, "col"),
        P(None, "col"),
        P("col", "row"),
        P("row"),
        P("row", "col"),
        P("col"),
        P("col", "row"),
        P("row"),
    )
    out_specs = (
        P(("dp", "col"), "row"),
        P(("dp", "col"), "row"),
        P(None, "col"),
        P("col", None, "row"),
        P(None, "row"),
        P("row", None, "col"),
        P(None, "col"),
        P("col", "row"),
        P("row"),
        P("row", "col"),
        P("col"),
        P("col", "row"),
        P("row"),
    )
    return jax.shard_map(shards, mesh=mesh, in_specs=in_specs, out_specs=out_specs, check_vma=False)
```

```python
from functools import partial
import math

import jax
import jax.numpy as jnp
from jax import lax
from jax.experimental import pallas as pl
from jax.experimental.layout import Layout, with_layout_constraint
from jax.experimental.pallas import tpu as pltpu
from jax.sharding import PartitionSpec as P

HD = 72
norm_epsilon = 1e-06
fast_mode = lax.Precision.HIGH
exact_mode = lax.Precision.HIGHEST


def contract(left, right, left_dim, right_dim, precision=fast_mode):
    return lax.dot_general(
        left,
        right,
        (((left_dim,), (right_dim,)), ((), ())),
        precision=precision,
        preferred_element_type=jnp.float32,
    )


def row_major(values):
    return with_layout_constraint(values, Layout(major_to_minor=tuple(range(values.ndim))))


def shift_row(values, step):
    count = lax.axis_size("row")
    if step % count == 0:
        return values
    return lax.ppermute(values, "row", [(i, (i + step) % count) for i in range(count)])


def shift_chip(values, step):
    count = lax.axis_size("col") // 2
    if step % count == 0:
        return values
    pairs = [
        (2 * i + core, 2 * ((i + step) % count) + core) for i in range(count) for core in range(2)
    ]
    return lax.ppermute(values, "col", pairs)


def swap_core(values):
    return lax.ppermute(values, "col", [(i, i ^ 1) for i in range(lax.axis_size("col"))])


def swap_dp(values):
    return lax.ppermute(values, "dp", [(0, 1), (1, 0)])


def butterfly(values, axis):
    count = lax.axis_size(axis)
    step = 1
    while step < count:
        values = values + lax.ppermute(values, axis, [(i, i ^ step) for i in range(count)])
        step *= 2
    return values


def row_order():
    count = lax.axis_size("row")
    return sorted(range(count), key=lambda step: (min(step, count - step), step))


def spread(block):
    count = lax.axis_size("row")
    chips = lax.axis_size("col") // 2
    by_step = {0: block}
    for step in row_order()[1:]:
        if step <= count // 2:
            by_step[step] = shift_row(by_step[step - 1], 1)
        else:
            by_step[step] = shift_row(by_step[(step + 1) % count], -1)
    groups = []
    for step in row_order():
        groups.append([shift_chip(by_step[step], chip) for chip in range(chips)])
    near = jnp.concatenate(sum(groups[:-1], []), axis=0)
    far = jnp.concatenate(groups[-1], axis=0)
    return [near, far, swap_core(near), swap_core(far)]


def by_piece(function, pieces):
    return jnp.concatenate([function(piece) for piece in pieces], axis=0)


def scatter_tokens(partial_rows, tokens, fill):
    count = lax.axis_size("row")
    chips = lax.axis_size("col") // 2
    half = tokens // 2
    group = half // count
    size = group // chips
    split = half - group
    far = swap_core(partial_rows(half + split, group))
    near = swap_core(partial_rows(half, split))
    far = partial_rows(split, group) + far
    near = partial_rows(0, split) + near
    filled = fill(near)
    sums = {}
    for place, step in reversed(list(enumerate(row_order()))):
        part = far if place == count - 1 else near[place * group : (place + 1) * group]
        total = part[:size]
        for chip in range(1, chips):
            total = total + shift_chip(part[chip * size : (chip + 1) * size], -chip)
        sums[step] = total
    for step in reversed(row_order()[1:]):
        if step <= count // 2:
            sums[step - 1] = sums[step - 1] + shift_row(sums[step], -1)
        else:
            back = (step + 1) % count
            sums[back] = sums[back] + shift_row(sums[step], 1)
    return sums[0], filled


def after(values, earlier):
    return lax.optimization_barrier((values, earlier))[0]


def copy_blocks(size, places_ref, source_ref, target_ref):
    def body(block, carry):
        start = pl.multiple_of(places_ref[block] * size, 8)
        target = pl.multiple_of(block * size, 8)
        target_ref[pl.ds(target, size), :] = source_ref[pl.ds(start, size), :]
        return carry

    lax.fori_loop(0, places_ref.shape[0], body, 0)


def take_blocks(values, places):
    size = values.shape[0] // places.shape[0]
    return pl.pallas_call(
        partial(copy_blocks, size),
        in_specs=[
            pl.BlockSpec(memory_space=pltpu.SMEM),
            pl.BlockSpec(memory_space=pltpu.VMEM),
        ],
        out_specs=pl.BlockSpec(memory_space=pltpu.VMEM),
        out_shape=jax.ShapeDtypeStruct(values.shape, values.dtype),
        cost_estimate=pl.CostEstimate(flops=0, transcendentals=0, bytes_accessed=8 * values.size),
        name="take_blocks",
    )(places, values)


def block_places():
    rows, cols = lax.axis_size("row"), lax.axis_size("col")
    chips = cols // 2
    me_row, me_col = lax.axis_index("row"), lax.axis_index("col")
    tokens_mesh = []
    for core in range(2):
        for step in row_order():
            for chip in range(chips):
                col = (me_col // 2 - chip) % chips * 2 + (me_col % 2 + core) % 2
                tokens_mesh.append(col * rows + (me_row - step) % rows)
    tokens_mesh = jnp.stack(tokens_mesh).astype(jnp.int32)
    numbers = jnp.arange(rows * cols, dtype=jnp.int32)
    mesh_tokens = jnp.sum(
        jnp.where(tokens_mesh[None, :] == numbers[:, None], numbers[None, :], 0), axis=1
    )
    return tokens_mesh, mesh_tokens


def gather_mesh(local):
    return lax.all_gather(local, ("col", "row"), axis=0, tiled=True)


def scatter_mesh(partial_sums):
    return lax.psum_scatter(partial_sums, ("col", "row"), scatter_dimension=0, tiled=True)


def row_parts(blocks):
    count = lax.axis_size("row")
    me = lax.axis_index("row")
    return [
        shift_row(lax.dynamic_index_in_dim(blocks, (me + step) % count, 0, keepdims=False), step)
        for step in range(count)
    ]


def by_source(parts):
    count = lax.axis_size("row")
    me = lax.axis_index("row")
    stacked = jnp.stack(parts)
    return [
        lax.dynamic_index_in_dim(stacked, (me - row) % count, 0, keepdims=False)
        for row in range(count)
    ]


def move_rows(blocks):
    return row_major(jnp.stack(row_parts(row_major(blocks))))


def own_half(blocks, axis):
    if lax.axis_size("dp") != 2:
        return blocks
    half = blocks.shape[axis] // 2
    return lax.dynamic_slice_in_dim(blocks, lax.axis_index("dp") * half, half, axis)


def share_blocks(mine):
    if lax.axis_size("dp") != 2:
        return mine[None]
    return jnp.stack([mine, swap_dp(mine)])


def order_blocks(both):
    if lax.axis_size("dp") != 2:
        return by_source(list(both[0]))
    me = lax.axis_index("dp")
    low = by_source(list(lax.dynamic_index_in_dim(both, me, 0, keepdims=False)))
    high = by_source(list(lax.dynamic_index_in_dim(both, 1 - me, 0, keepdims=False)))
    return [jnp.concatenate(pair, axis=0) for pair in zip(low, high)]


def whole_blocks(mine):
    return order_blocks(share_blocks(mine))


def pair_total(grad):
    count = lax.axis_size("row")
    rows = grad.shape[0] // count
    if lax.axis_size("dp") != 2:
        total = lax.psum(grad, "dp").reshape(count, rows, grad.shape[1])
        return total, jnp.zeros_like(total)
    me = lax.axis_index("dp")
    halves = row_major(grad.reshape(count, 2, rows // 2, grad.shape[1]))
    given = lax.dynamic_index_in_dim(halves, 1 - me, 1, keepdims=False)
    kept = lax.dynamic_index_in_dim(halves, me, 1, keepdims=False)
    return kept, swap_dp(given)


def dp_stack(values):
    if lax.axis_size("dp") == 2:
        both = jnp.stack([values, swap_dp(values)])
        me = lax.axis_index("dp")
        return jnp.stack(
            [
                lax.dynamic_index_in_dim(both, me, 0, keepdims=False),
                lax.dynamic_index_in_dim(both, 1 - me, 0, keepdims=False),
            ]
        )
    return lax.all_gather(values, "dp", axis=0, tiled=False)


def normalize(values):
    center = jnp.mean(values, axis=1, keepdims=True)
    centred = values - center
    spread_of = jnp.mean(centred * centred, axis=1, keepdims=True)
    inverse = lax.rsqrt(spread_of + norm_epsilon)
    return (centred * inverse, inverse)


def normalize_back(grad_values, normed, inverse):
    totals = jnp.mean(grad_values, axis=1, keepdims=True)
    along = jnp.mean(grad_values * normed, axis=1, keepdims=True)
    return inverse * (grad_values - totals - normed * along)


def shards(
    block_in,
    labels,
    steps_t,
    out_cot,
    class_table,
    w_ada,
    b_ada,
    w_qkv,
    b_qv,
    w_out,
    b_out,
    w_up,
    b_up,
    w_down,
    b_down,
):
    rows = lax.axis_size("row")
    me_row = lax.axis_index("row")
    me_col = lax.axis_index("col")
    tok_local, width_row = block_in.shape
    width = width_row * rows
    width_col = w_out.shape[0]
    heads_col = width_col // HD
    heads_own = max(1, heads_col // rows)
    copies = max(1, rows // heads_col)
    head_width = heads_own * HD
    head_groups = rows // copies
    units_own = w_up.shape[1] // rows

    tokens_mesh, mesh_tokens = block_places()
    tokens = tok_local * lax.axis_size("col")

    qkv_blocks = (
        w_qkv.reshape(width_row, 3, head_groups, head_width)
        .transpose(2, 0, 1, 3)
        .reshape(head_groups, width_row, 3 * head_width)
    )
    out_blocks = w_out.reshape(head_groups, head_width, width_row).transpose(0, 2, 1)
    head_blocks = jnp.concatenate([qkv_blocks, out_blocks], axis=2)
    head_blocks = own_half(jnp.repeat(head_blocks, copies, axis=0), 1)

    feature = me_col * width_col + jnp.arange(width_col)
    half_width = width // 2
    frequency = jnp.exp(
        -math.log(10000.0) * (feature % half_width).astype(jnp.float32) / half_width
    )
    angles = steps_t.astype(jnp.float32)[:, None] * frequency[None, :]
    own_class = lax.dynamic_slice_in_dim(class_table, labels[0], 1, 0)
    condition = own_class + jnp.where(
        feature[None, :] < half_width, jnp.cos(angles), jnp.sin(angles)
    )
    silu_cond, silu_pull = jax.vjp(jax.nn.silu, condition)
    ada_terms = jnp.sum(silu_cond[0][:, None, None] * w_ada, axis=0)
    head_blocks = move_rows(after(head_blocks, ada_terms))
    ada_terms = butterfly(ada_terms, "col") + b_ada
    small = jnp.concatenate([ada_terms, b_out[None], b_down[None]], axis=0)
    small = by_source([shift_row(small, step) for step in range(rows)])
    small = jnp.concatenate(small, axis=1)[:, None, :]
    shift_one, scale_one, gate_one, shift_two, scale_two, gate_two, out_bias, down_bias = small

    both_own = row_parts(
        jnp.concatenate([block_in, out_cot], axis=1).reshape(
            rows, tok_local // rows, 2 * width_row
        )
    )
    both_own = by_source(both_own)
    in_own = jnp.concatenate([part[:, :width_row] for part in both_own], axis=1)
    cot_own = jnp.concatenate([part[:, width_row:] for part in both_own], axis=1)
    in_pieces = spread(in_own)
    head_blocks = after(head_blocks, in_own)
    head_matrix = jnp.concatenate(whole_blocks(head_blocks), axis=0)
    qkv_matrix = head_matrix[:, : 3 * head_width]
    out_flip = head_matrix[:, 3 * head_width :]
    normed_one, inverse_one = normalize(in_own)
    hidden_one = [normalize(piece)[0] * (1.0 + scale_one) + shift_one for piece in in_pieces]
    head_start = (me_row // copies) * head_width
    head_bias = lax.dynamic_slice_in_dim(b_qv, head_start, head_width, 1)
    qkv = by_piece(lambda piece: contract(piece, qkv_matrix, 1, 0), hidden_one)
    qkv = qkv.reshape(tokens, 3, heads_own, HD)
    queries = qkv[:, 0] + head_bias[0].reshape(heads_own, HD)
    keys = qkv[:, 1]
    values = qkv[:, 2] + head_bias[1].reshape(heads_own, HD)
    factor = 1.0 / math.sqrt(HD)
    scores = jnp.einsum("qhd,khd->hqk", queries, keys, precision=fast_mode) * factor
    weights = jnp.exp(scores)
    weights = weights / jnp.sum(weights, axis=2, keepdims=True)
    attended = jnp.einsum("hqk,khd->qhd", weights, values, precision=fast_mode)
    attended = attended.reshape(tokens, head_width)

    mlp_blocks = jnp.stack(
        [
            jnp.concatenate(
                [
                    w_up[:, i * units_own : (i + 1) * units_own],
                    w_down[i * units_own : (i + 1) * units_own].T,
                ],
                axis=1,
            )
            for i in range(rows)
        ]
    )
    mlp_blocks = move_rows(after(own_half(mlp_blocks, 1), in_pieces[3]))
    attn_out, mlp_blocks = scatter_tokens(
        lambda start, size: contract(attended[start : start + size], out_flip, 1, 1)
        * (1.0 / copies),
        tokens,
        lambda earlier: share_blocks(after(mlp_blocks, earlier)),
    )
    attn_out = attn_out + out_bias
    mixed = in_own + gate_one * attn_out
    normed_two, inverse_two = normalize(mixed)
    hidden_two_own = normed_two * (1.0 + scale_two) + shift_two
    hidden_two = spread(hidden_two_own)

    d_mlp_own = cot_own * gate_two
    d_mlp = gather_mesh(after(cot_own, in_pieces[3])) * gate_two
    mlp_matrix = jnp.concatenate(order_blocks(after(mlp_blocks, hidden_two_own)), axis=0)
    up_matrix = mlp_matrix[:, :units_own]
    down_matrix = mlp_matrix[:, units_own:]
    up_bias = lax.dynamic_slice_in_dim(b_up, me_row * units_own, units_own, 0)
    up_values = by_piece(lambda piece: contract(piece, up_matrix, 1, 0), hidden_two) + up_bias
    activated, gelu_pull = jax.vjp(partial(jax.nn.gelu, approximate=True), up_values)
    d_activated = take_blocks(contract(d_mlp, down_matrix, 1, 0), tokens_mesh)
    (d_up,) = gelu_pull(d_activated)

    def mlp_rest(earlier):
        activated_mesh = take_blocks(after(activated, earlier), mesh_tokens)
        up_grad = contract(jnp.concatenate(after(hidden_two, earlier)), d_up, 0, 0)
        down_grad = contract(d_mlp, activated_mesh, 0, 0)
        return activated_mesh, jnp.concatenate([up_grad, down_grad], axis=1)

    d_hidden_two, (activated_mesh, mlp_grad) = scatter_tokens(
        lambda start, size: contract(d_up[start : start + size], up_matrix, 1, 1),
        tokens,
        mlp_rest,
    )

    d_mixed = cot_own + normalize_back(d_hidden_two * (1.0 + scale_two), normed_two, inverse_two)
    d_attn_own = d_mixed * gate_one
    d_attn = spread(d_attn_own)
    mlp_part = contract(after(activated_mesh, d_attn_own), down_matrix, 1, 1)
    mlp_own = scatter_mesh(mlp_part) + down_bias
    mlp_kept, mlp_given = pair_total(after(mlp_grad, d_attn_own))
    d_attended = by_piece(lambda piece: contract(piece, out_flip, 1, 0), d_attn)
    d_attended = d_attended.reshape(tokens, heads_own, HD)
    mlp_kept, mlp_given = after((mlp_kept, mlp_given), d_attended)
    mlp_moved = move_rows(mlp_kept + mlp_given)
    d_weights = jnp.einsum("qhd,khd->hqk", d_attended, values, precision=fast_mode)
    row_dots = jnp.sum(weights * d_weights, axis=2, keepdims=True)
    d_scores = weights * (d_weights - row_dots) * factor
    d_query = jnp.einsum("hqk,khd->qhd", d_scores, keys, precision=fast_mode)
    d_key = jnp.einsum("hqk,qhd->khd", d_scores, queries, precision=fast_mode)
    d_value = jnp.einsum("hqk,qhd->khd", weights, d_attended, precision=fast_mode)
    d_qkv = jnp.stack([d_query, d_key, d_value], axis=1).reshape(tokens, 3 * head_width)

    def head_rest(earlier):
        mlp_shared = share_blocks(after(mlp_moved, earlier))
        d_heads = after(d_qkv, earlier)
        qkv_grad = contract(jnp.concatenate(hidden_one), d_heads, 0, 0)
        out_grad = contract(jnp.concatenate(d_attn), after(attended, earlier), 0, 0)
        return mlp_shared, pair_total(jnp.concatenate([qkv_grad, out_grad], axis=1))

    d_hidden_one, (mlp_shared, head_grad) = scatter_tokens(
        lambda start, size: contract(d_qkv[start : start + size], qkv_matrix, 1, 1)
        * (1.0 / copies),
        tokens,
        head_rest,
    )
    head_kept, head_given = after(head_grad, d_hidden_one)
    head_grad = head_kept + head_given
    head_grad = whole_blocks(move_rows(head_grad))[::copies]
    qkv_grad = jnp.stack(
        [part[:, : 3 * head_width].reshape(width_row, 3, head_width) for part in head_grad],
        axis=2,
    ).reshape(width_row, 3, width_col)
    out_grad = jnp.concatenate([part[:, 3 * head_width :].T for part in head_grad], axis=0)
    mlp_grad = order_blocks(after(mlp_shared, d_hidden_one))
    mlp_own = after(mlp_own, d_hidden_one)
    up_grad = jnp.concatenate([part[:, :units_own] for part in mlp_grad], axis=1)
    down_grad = jnp.concatenate([part[:, units_own:].T for part in mlp_grad], axis=0)

    in_grad = d_mixed + normalize_back(
        d_hidden_one * (1.0 + scale_one), normed_one, inverse_one
    )
    block_out = mixed + gate_two * mlp_own
    results = jnp.stack(
        [
            jnp.concatenate(
                [
                    block_out[:, i * width_row : (i + 1) * width_row],
                    in_grad[:, i * width_row : (i + 1) * width_row],
                ],
                axis=1,
            )
            for i in range(rows)
        ]
    )
    results = jnp.concatenate(by_source(row_parts(results)), axis=0)

    unit_sums = jnp.concatenate([jnp.sum(d_up, axis=0), jnp.sum(d_qkv, axis=0)])
    unit_sums = jnp.stack(by_source([shift_row(unit_sums, step) for step in range(rows)]))
    own_sums = jnp.stack(
        [
            jnp.sum(d_hidden_one, axis=0),
            jnp.sum(d_hidden_one * normed_one, axis=0),
            jnp.sum(d_mixed * attn_out, axis=0),
            jnp.sum(d_hidden_two, axis=0),
            jnp.sum(d_hidden_two * normed_two, axis=0),
            jnp.sum(cot_own * mlp_own, axis=0),
            jnp.sum(d_attn_own, axis=0),
            jnp.sum(d_mlp_own, axis=0),
        ]
    )
    own_sums = butterfly(butterfly(own_sums, "col"), "row")
    own_sums = lax.dynamic_slice_in_dim(own_sums, me_row * width_row, width_row, 1)
    label_row = jnp.broadcast_to(labels.astype(jnp.float32), (128,))
    unit_size = unit_sums.size
    pack = dp_stack(
        jnp.concatenate([unit_sums.reshape(-1), own_sums.reshape(-1), silu_cond[0], label_row])
    )
    unit_sums = jnp.sum(pack[:, :unit_size], axis=0).reshape(rows, -1)
    up_bias_grad = unit_sums[:, :units_own].reshape(-1)
    qkv_sums = unit_sums[::copies, units_own:].reshape(head_groups, 3, head_width)
    qv_bias_grad = jnp.stack([qkv_sums[:, 0].reshape(-1), qkv_sums[:, 2].reshape(-1)])
    sums_all = pack[:, unit_size : unit_size + 8 * width_row].reshape(-1, 8, width_row)
    silu_all = pack[:, unit_size + 8 * width_row : -128]
    bias_sums = jnp.sum(sums_all, axis=0)
    ada_grad = jnp.sum(silu_all[:, :, None, None] * sums_all[:, None, :6], axis=0)
    silu_grads = jnp.sum(own_sums[None, :6] * w_ada, axis=(1, 2))[None]
    silu_grads = butterfly(silu_grads, "row")
    (cond_grad,) = silu_pull(silu_grads)
    cond_all = dp_stack(cond_grad[0])
    label_all = pack[:, -1].astype(jnp.int32)
    classes = jnp.arange(class_table.shape[0])
    table_grad = jnp.sum(
        jnp.where(
            label_all[:, None, None] == classes[None, :, None], cond_all[:, None, :], 0.0
        ),
        axis=0,
    )
    return (
        results[:, :width_row],
        results[:, width_row:],
        table_grad,
        ada_grad,
        bias_sums[:6],
        qkv_grad,
        qv_bias_grad,
        out_grad,
        bias_sums[6],
        up_grad,
        up_bias_grad,
        down_grad,
        bias_sums[7],
    )


def solution(mesh):
    in_specs = (
        P(("dp", "col"), "row"),
        P("dp"),
        P("dp"),
        P(("dp", "col"), "row"),
        P(None, "col"),
        P("col", None, "row"),
        P(None, "row"),
        P("row", None, "col"),
        P(None, "col"),
        P("col", "row"),
        P("row"),
        P("row", "col"),
        P("col"),
        P("col", "row"),
        P("row"),
    )
    out_specs = (
        P(("dp", "col"), "row"),
        P(("dp", "col"), "row"),
        P(None, "col"),
        P("col", None, "row"),
        P(None, "row"),
        P("row", None, "col"),
        P(None, "col"),
        P("col", "row"),
        P("row"),
        P("row", "col"),
        P("col"),
        P("col", "row"),
        P("row"),
    )
    return jax.shard_map(shards, mesh=mesh, in_specs=in_specs, out_specs=out_specs, check_vma=False)
```

```python
from functools import partial
import math

import jax
import jax.numpy as jnp
from jax import lax
from jax.experimental import pallas as pl
from jax.experimental.layout import Layout, with_layout_constraint
from jax.experimental.pallas import tpu as pltpu
from jax.sharding import PartitionSpec as P


HD = 72
norm_epsilon = 1e-06
fast_mode = lax.Precision.HIGH


def contract(left, right, left_dim, right_dim, precision=fast_mode):
    return lax.dot_general(
        left,
        right,
        (((left_dim,), (right_dim,)), ((), ())),
        precision=precision,
        preferred_element_type=jnp.float32,
    )


def row_major(values):
    return with_layout_constraint(values, Layout(major_to_minor=tuple(range(values.ndim))))


def shift_row(values, step):
    count = lax.axis_size("row")
    if step % count == 0:
        return values
    return lax.ppermute(values, "row", [(i, (i + step) % count) for i in range(count)])


def shift_chip(values, step):
    count = lax.axis_size("col") // 2
    if step % count == 0:
        return values
    pairs = [
        (2 * i + core, 2 * ((i + step) % count) + core) for i in range(count) for core in range(2)
    ]
    return lax.ppermute(values, "col", pairs)


def swap_core(values):
    return lax.ppermute(values, "col", [(i, i ^ 1) for i in range(lax.axis_size("col"))])


def swap_dp(values):
    return lax.ppermute(values, "dp", [(0, 1), (1, 0)])


def butterfly(values, axis):
    count = lax.axis_size(axis)
    step = 1
    while step < count:
        values = values + lax.ppermute(values, axis, [(i, i ^ step) for i in range(count)])
        step *= 2
    return values


def row_order():
    count = lax.axis_size("row")
    return sorted(range(count), key=lambda step: (min(step, count - step), step))


def spread(block, ready=()):
    count = lax.axis_size("row")
    chips = lax.axis_size("col") // 2
    by_step = {0: block}
    own_chips = [shift_chip(block, chip) for chip in range(chips)]
    for step in row_order()[1:-1]:
        if step <= count // 2:
            by_step[step] = shift_row(by_step[step - 1], 1)
        else:
            by_step[step] = shift_row(by_step[(step + 1) % count], -1)
    by_step, ready = lax.optimization_barrier((by_step, ready))
    last = row_order()[-1]
    by_step[last] = shift_row(by_step[last - 1], 1)
    groups = [own_chips]
    for step in row_order()[1:]:
        groups.append([shift_chip(by_step[step], chip) for chip in range(chips)])
    near = jnp.concatenate(sum(groups[:-1], []), axis=0)
    far = jnp.concatenate(groups[-1], axis=0)
    return [near, far, swap_core(near), swap_core(far)], ready


def by_piece(function, pieces):
    return jnp.concatenate([function(piece) for piece in pieces], axis=0)


def scatter_tokens(partial_rows, tokens, fill, fill_row=lambda earlier, value: value):
    count = lax.axis_size("row")
    chips = lax.axis_size("col") // 2
    half = tokens // 2
    group = half // count
    size = group // chips
    split = half - group
    far = swap_core(partial_rows(half + split, group))
    near = swap_core(partial_rows(half, split))
    far = partial_rows(split, group) + far
    near = partial_rows(0, split) + near
    filled = fill(near)
    sums = {}
    for place, step in reversed(list(enumerate(row_order()))):
        part = far if place == count - 1 else near[place * group : (place + 1) * group]
        total = part[:size]
        for chip in range(1, chips):
            total = total + shift_chip(part[chip * size : (chip + 1) * size], -chip)
        sums[step] = total
    filled = fill_row(sums[1], filled)
    for step in reversed(row_order()[1:]):
        if step <= count // 2:
            sums[step - 1] = sums[step - 1] + shift_row(sums[step], -1)
        else:
            back = (step + 1) % count
            sums[back] = sums[back] + shift_row(sums[step], 1)
    return sums[0], filled


def after(values, earlier):
    return lax.optimization_barrier((values, earlier))[0]


def copy_blocks(size, places_ref, source_ref, target_ref):
    def body(block, carry):
        start = pl.multiple_of(places_ref[block] * size, 8)
        target = pl.multiple_of(block * size, 8)
        target_ref[pl.ds(target, size), :] = source_ref[pl.ds(start, size), :]
        return carry

    lax.fori_loop(0, places_ref.shape[0], body, 0)


def take_blocks(values, places):
    size = values.shape[0] // places.shape[0]
    return pl.pallas_call(
        partial(copy_blocks, size),
        in_specs=[
            pl.BlockSpec(memory_space=pltpu.SMEM),
            pl.BlockSpec(memory_space=pltpu.VMEM),
        ],
        out_specs=pl.BlockSpec(memory_space=pltpu.VMEM),
        out_shape=jax.ShapeDtypeStruct(values.shape, values.dtype),
        cost_estimate=pl.CostEstimate(flops=0, transcendentals=0, bytes_accessed=8 * values.size),
        name="take_blocks",
    )(places, values)


def block_places():
    rows, cols = lax.axis_size("row"), lax.axis_size("col")
    chips = cols // 2
    me_row, me_col = lax.axis_index("row"), lax.axis_index("col")
    tokens_mesh = []
    for core in range(2):
        for step in row_order():
            for chip in range(chips):
                col = (me_col // 2 - chip) % chips * 2 + (me_col % 2 + core) % 2
                tokens_mesh.append(col * rows + (me_row - step) % rows)
    tokens_mesh = jnp.stack(tokens_mesh).astype(jnp.int32)
    numbers = jnp.arange(rows * cols, dtype=jnp.int32)
    mesh_tokens = jnp.sum(
        jnp.where(tokens_mesh[None, :] == numbers[:, None], numbers[None, :], 0), axis=1
    )
    return tokens_mesh, mesh_tokens


def gather_mesh(local):
    return lax.all_gather(local, ("col", "row"), axis=0, tiled=True)


def scatter_mesh(partial_sums):
    return lax.psum_scatter(partial_sums, ("col", "row"), scatter_dimension=0, tiled=True)


def row_outgoing(blocks):
    count = lax.axis_size("row")
    me = lax.axis_index("row")
    return [
        lax.dynamic_index_in_dim(blocks, (me + step) % count, 0, keepdims=False)
        for step in range(count)
    ]


def row_send(outgoing):
    return [shift_row(block, step) for step, block in enumerate(outgoing)]


def row_parts(blocks):
    return row_send(row_outgoing(blocks))


def by_source(parts):
    count = lax.axis_size("row")
    me = lax.axis_index("row")
    stacked = jnp.stack(parts)
    return [
        lax.dynamic_index_in_dim(stacked, (me - row) % count, 0, keepdims=False)
        for row in range(count)
    ]


def move_rows(blocks):
    return row_major(jnp.stack(row_parts(row_major(blocks))))


def own_half(blocks, axis):
    if lax.axis_size("dp") != 2:
        return blocks
    half = blocks.shape[axis] // 2
    return lax.dynamic_slice_in_dim(blocks, lax.axis_index("dp") * half, half, axis)


def share_blocks(mine):
    if lax.axis_size("dp") != 2:
        return mine[None]
    return jnp.stack([mine, swap_dp(mine)])


def order_blocks(both):
    if lax.axis_size("dp") != 2:
        return by_source(list(both[0]))
    me = lax.axis_index("dp")
    low = by_source(list(lax.dynamic_index_in_dim(both, me, 0, keepdims=False)))
    high = by_source(list(lax.dynamic_index_in_dim(both, 1 - me, 0, keepdims=False)))
    return [jnp.concatenate(pair, axis=0) for pair in zip(low, high)]


def pair_halves(grad):
    count = lax.axis_size("row")
    rows = grad.shape[0] // count
    if lax.axis_size("dp") != 2:
        total = grad.reshape(count, rows, grad.shape[1])
        return jnp.zeros_like(total), total
    me = lax.axis_index("dp")
    halves = row_major(grad.reshape(count, 2, rows // 2, grad.shape[1]))
    given = lax.dynamic_index_in_dim(halves, 1 - me, 1, keepdims=False)
    kept = lax.dynamic_index_in_dim(halves, me, 1, keepdims=False)
    return row_major(kept), row_major(given)


def pair_swap(given):
    return swap_dp(given) if lax.axis_size("dp") == 2 else lax.psum(given, "dp")


def dp_stack(values):
    if lax.axis_size("dp") == 2:
        both = jnp.stack([values, swap_dp(values)])
        me = lax.axis_index("dp")
        return jnp.stack(
            [
                lax.dynamic_index_in_dim(both, me, 0, keepdims=False),
                lax.dynamic_index_in_dim(both, 1 - me, 0, keepdims=False),
            ]
        )
    return lax.all_gather(values, "dp", axis=0, tiled=False)


def normalize(values):
    center = jnp.mean(values, axis=1, keepdims=True)
    centred = values - center
    spread_of = jnp.mean(centred * centred, axis=1, keepdims=True)
    inverse = lax.rsqrt(spread_of + norm_epsilon)
    return (centred * inverse, inverse)


def normalize_back(grad_values, normed, inverse):
    totals = jnp.mean(grad_values, axis=1, keepdims=True)
    along = jnp.mean(grad_values * normed, axis=1, keepdims=True)
    return inverse * (grad_values - totals - normed * along)


def shards(
    block_in,
    labels,
    steps_t,
    out_cot,
    class_table,
    w_ada,
    b_ada,
    w_qkv,
    b_qv,
    w_out,
    b_out,
    w_up,
    b_up,
    w_down,
    b_down,
):
    rows = lax.axis_size("row")
    me_row = lax.axis_index("row")
    me_col = lax.axis_index("col")
    tok_local, width_row = block_in.shape
    width = width_row * rows
    width_col = w_out.shape[0]
    heads_col = width_col // HD
    heads_own = max(1, heads_col // rows)
    copies = max(1, rows // heads_col)
    head_width = heads_own * HD
    head_groups = rows // copies
    units_own = w_up.shape[1] // rows

    tokens_mesh, mesh_tokens = block_places()
    tokens = tok_local * lax.axis_size("col")

    feature = me_col * width_col + jnp.arange(width_col)
    half_width = width // 2
    frequency = jnp.exp(
        -math.log(10000.0) * (feature % half_width).astype(jnp.float32) / half_width
    )
    angles = steps_t.astype(jnp.float32)[:, None] * frequency[None, :]
    own_class = lax.dynamic_slice_in_dim(class_table, labels[0], 1, 0)
    condition = own_class + jnp.where(
        feature[None, :] < half_width, jnp.cos(angles), jnp.sin(angles)
    )
    silu_cond, silu_pull = jax.vjp(jax.nn.silu, condition)
    both_own = row_parts(
        jnp.concatenate([block_in, out_cot], axis=1).reshape(
            rows, tok_local // rows, 2 * width_row
        )
    )
    both_own = by_source(both_own)
    in_own = jnp.concatenate([part[:, :width_row] for part in both_own], axis=1)
    cot_own = jnp.concatenate([part[:, width_row:] for part in both_own], axis=1)
    silu_now, qkv_now, out_now, up_now, down_now = after(
        (silu_cond, w_qkv, w_out, w_up, w_down), in_own
    )
    ada_terms = jnp.sum(silu_now[0][:, None, None] * w_ada, axis=0)

    qkv_blocks = (
        qkv_now.reshape(width_row, 3, head_groups, head_width)
        .transpose(2, 0, 1, 3)
        .reshape(head_groups, width_row, 3 * head_width)
    )
    out_blocks = out_now.reshape(head_groups, head_width, width_row).transpose(0, 2, 1)
    head_blocks = jnp.concatenate([qkv_blocks, out_blocks], axis=2)
    head_blocks = own_half(jnp.repeat(head_blocks, copies, axis=0), 1)
    mlp_blocks = own_half(
        jnp.stack(
            [
                jnp.concatenate(
                    [
                        up_now[:, i * units_own : (i + 1) * units_own],
                        down_now[i * units_own : (i + 1) * units_own].T,
                    ],
                    axis=1,
                )
                for i in range(rows)
            ]
        ),
        1,
    )
    mlp_sent = row_outgoing(mlp_blocks)
    in_pieces, mlp_sent = spread(in_own, mlp_sent)
    ada_terms = butterfly(ada_terms, "col") + b_ada
    head_blocks = move_rows(head_blocks)
    mlp_blocks = row_major(jnp.stack(row_send(mlp_sent)))
    small = jnp.concatenate([ada_terms, b_out[None], b_down[None]], axis=0)
    small = [shift_row(small, step) for step in range(rows)]
    small = by_source(after(small, in_pieces[1]))
    small = jnp.concatenate(small, axis=1)[:, None, :]
    shift_one, scale_one, gate_one, shift_two, scale_two, gate_two, out_bias, down_bias = small

    head_blocks = share_blocks(head_blocks)
    head_matrix = jnp.concatenate(order_blocks(after(head_blocks, in_pieces[1])), axis=0)
    qkv_matrix = head_matrix[:, : 3 * head_width]
    out_flip = head_matrix[:, 3 * head_width :]
    normed_one, inverse_one = normalize(in_own)
    hidden_one = [normalize(piece)[0] * (1.0 + scale_one) + shift_one for piece in in_pieces]
    head_start = (me_row // copies) * head_width
    head_bias = lax.dynamic_slice_in_dim(b_qv, head_start, head_width, 1)
    qkv = by_piece(lambda piece: contract(piece, qkv_matrix, 1, 0), hidden_one)
    qkv = qkv.reshape(tokens, 3, heads_own, HD)
    queries = qkv[:, 0] + head_bias[0].reshape(heads_own, HD)
    keys = qkv[:, 1]
    values = qkv[:, 2] + head_bias[1].reshape(heads_own, HD)
    factor = 1.0 / math.sqrt(HD)
    scores = jnp.einsum("qhd,khd->hqk", queries, keys, precision=fast_mode) * factor
    weights = jnp.exp(scores)
    weights = weights / jnp.sum(weights, axis=2, keepdims=True)
    attended = jnp.einsum("hqk,khd->qhd", weights, values, precision=fast_mode)
    attended = attended.reshape(tokens, head_width)

    def share_mlp(earlier):
        return share_blocks(after(mlp_blocks, earlier))

    attn_out, mlp_blocks = scatter_tokens(
        lambda start, size: contract(attended[start : start + size], out_flip, 1, 1)
        * (1.0 / copies),
        tokens,
        share_mlp,
    )
    attn_out = attn_out + out_bias
    mixed = in_own + gate_one * attn_out
    normed_two, inverse_two = normalize(mixed)
    hidden_two_own = normed_two * (1.0 + scale_two) + shift_two
    mlp_matrix = row_major(
        jnp.concatenate(order_blocks(after(mlp_blocks, hidden_two_own)), axis=0)
    )
    up_matrix = mlp_matrix[:, :units_own]
    down_matrix = mlp_matrix[:, units_own:]

    d_mlp_own = cot_own * gate_two
    cot_all = gather_mesh(after(cot_own, in_pieces[1]))
    d_activated = contract(cot_all, gate_two.reshape(width, 1) * down_matrix, 1, 0)
    d_activated = take_blocks(d_activated, tokens_mesh)
    hidden_two, (up_matrix, down_matrix, d_activated) = spread(
        hidden_two_own, (up_matrix, down_matrix, d_activated)
    )
    up_bias = lax.dynamic_slice_in_dim(b_up, me_row * units_own, units_own, 0)
    up_values = by_piece(lambda piece: contract(piece, up_matrix, 1, 0), hidden_two) + up_bias
    activated, gelu_pull = jax.vjp(partial(jax.nn.gelu, approximate=True), up_values)
    (d_up,) = gelu_pull(d_activated)

    def mlp_rest(earlier):
        activated_mesh = take_blocks(after(activated, earlier), mesh_tokens)
        up_grad = contract(jnp.concatenate(after(hidden_two, earlier)), d_up, 0, 0)
        down_grad = contract(cot_all, activated_mesh, 0, 0) * gate_two.reshape(width, 1)
        halves = pair_halves(jnp.concatenate([up_grad, down_grad], axis=1))
        return contract(activated_mesh, down_matrix, 1, 1), halves

    d_hidden_two, mlp_rest_done = scatter_tokens(
        lambda start, size: contract(d_up[start : start + size], up_matrix, 1, 1), tokens, mlp_rest
    )

    d_mixed = cot_own + normalize_back(d_hidden_two * (1.0 + scale_two), normed_two, inverse_two)
    d_attn_own = d_mixed * gate_one
    d_attn, (mlp_part, (mlp_kept, mlp_given)) = spread(d_attn_own, mlp_rest_done)
    mlp_own = scatter_mesh(mlp_part)
    mlp_given = pair_swap(mlp_given)
    d_attended = by_piece(lambda piece: contract(piece, out_flip, 1, 0), d_attn)
    d_attended = d_attended.reshape(tokens, heads_own, HD)
    d_weights = jnp.einsum("qhd,khd->hqk", d_attended, values, precision=fast_mode)
    row_dots = jnp.sum(weights * d_weights, axis=2, keepdims=True)
    d_scores = weights * (d_weights - row_dots) * factor
    d_query = jnp.einsum("hqk,khd->qhd", d_scores, keys, precision=fast_mode)
    d_key = jnp.einsum("hqk,qhd->khd", d_scores, queries, precision=fast_mode)
    d_value = jnp.einsum("hqk,qhd->khd", weights, d_attended, precision=fast_mode)
    d_qkv = jnp.stack([d_query, d_key, d_value], axis=1).reshape(tokens, 3 * head_width)

    mlp_kept, mlp_given = after((mlp_kept, mlp_given), d_qkv)
    mlp_sent = row_outgoing(row_major(mlp_kept + mlp_given))

    def head_rest(earlier):
        mlp_moved = row_major(jnp.stack(row_send(after(mlp_sent, earlier))))
        d_heads = after(d_qkv, earlier)
        qkv_grad = contract(jnp.concatenate(hidden_one), d_heads, 0, 0)
        out_grad = contract(jnp.concatenate(d_attn), after(attended, earlier), 0, 0)
        kept, given = pair_halves(jnp.concatenate([qkv_grad, out_grad], axis=1))
        given = pair_swap(given)
        return mlp_moved, kept, given

    def head_rest_row(earlier, filled):
        mlp_moved, kept, given = filled
        return share_blocks(after(mlp_moved, earlier)), kept, given

    d_hidden_one, (mlp_shared, head_kept, head_given) = scatter_tokens(
        lambda start, size: contract(d_qkv[start : start + size], qkv_matrix, 1, 1)
        * (1.0 / copies),
        tokens,
        head_rest,
        head_rest_row,
    )
    mlp_own = after(mlp_own, d_hidden_one) + down_bias
    in_grad = d_mixed + normalize_back(
        d_hidden_one * (1.0 + scale_one), normed_one, inverse_one
    )
    block_out = mixed + gate_two * mlp_own
    results = jnp.stack(
        [
            jnp.concatenate(
                [
                    block_out[:, i * width_row : (i + 1) * width_row],
                    in_grad[:, i * width_row : (i + 1) * width_row],
                ],
                axis=1,
            )
            for i in range(rows)
        ]
    )
    results = row_parts(results)

    unit_sums = jnp.concatenate([jnp.sum(d_up, axis=0), jnp.sum(d_qkv, axis=0)])
    unit_sums = jnp.stack(by_source([shift_row(unit_sums, step) for step in range(rows)]))
    own_sums = jnp.stack(
        [
            jnp.sum(d_hidden_one, axis=0),
            jnp.sum(d_hidden_one * normed_one, axis=0),
            jnp.sum(d_mixed * attn_out, axis=0),
            jnp.sum(d_hidden_two, axis=0),
            jnp.sum(d_hidden_two * normed_two, axis=0),
            jnp.sum(cot_own * mlp_own, axis=0),
            jnp.sum(d_attn_own, axis=0),
            jnp.sum(d_mlp_own, axis=0),
        ]
    )
    own_sums = butterfly(own_sums, "col")
    head_kept, head_given = after((head_kept, head_given), own_sums)
    head_moved = move_rows(head_kept + head_given)
    own_sums = butterfly(own_sums, "row")
    head_grad = order_blocks(share_blocks(after(head_moved, own_sums)))[::copies]
    qkv_grad = jnp.stack(
        [part[:, : 3 * head_width].reshape(width_row, 3, head_width) for part in head_grad],
        axis=2,
    ).reshape(width_row, 3, width_col)
    out_grad = jnp.concatenate([part[:, 3 * head_width :].T for part in head_grad], axis=0)
    mlp_grad = order_blocks(after(mlp_shared, own_sums))
    up_grad = jnp.concatenate([part[:, :units_own] for part in mlp_grad], axis=1)
    down_grad = jnp.concatenate([part[:, units_own:].T for part in mlp_grad], axis=0)
    own_sums = lax.dynamic_slice_in_dim(own_sums, me_row * width_row, width_row, 1)
    results = jnp.concatenate(by_source(after(results, own_sums)), axis=0)
    label_row = jnp.broadcast_to(labels.astype(jnp.float32), (128,))
    unit_size = unit_sums.size
    pack = dp_stack(
        jnp.concatenate([unit_sums.reshape(-1), own_sums.reshape(-1), silu_cond[0], label_row])
    )
    unit_sums = jnp.sum(pack[:, :unit_size], axis=0).reshape(rows, -1)
    up_bias_grad = unit_sums[:, :units_own].reshape(-1)
    qkv_sums = unit_sums[::copies, units_own:].reshape(head_groups, 3, head_width)
    qv_bias_grad = jnp.stack([qkv_sums[:, 0].reshape(-1), qkv_sums[:, 2].reshape(-1)])
    sums_all = pack[:, unit_size : unit_size + 8 * width_row].reshape(-1, 8, width_row)
    silu_all = pack[:, unit_size + 8 * width_row : -128]
    bias_sums = jnp.sum(sums_all, axis=0)
    ada_grad = jnp.sum(silu_all[:, :, None, None] * sums_all[:, None, :6], axis=0)
    silu_grads = jnp.sum(own_sums[None, :6] * w_ada, axis=(1, 2))[None]
    silu_grads = butterfly(silu_grads, "row")
    (cond_grad,) = silu_pull(silu_grads)
    cond_all = dp_stack(cond_grad[0])
    label_all = pack[:, -1].astype(jnp.int32)
    classes = jnp.arange(class_table.shape[0])
    table_grad = jnp.sum(
        jnp.where(
            label_all[:, None, None] == classes[None, :, None], cond_all[:, None, :], 0.0
        ),
        axis=0,
    )
    return (
        results[:, :width_row],
        results[:, width_row:],
        table_grad,
        ada_grad,
        bias_sums[:6],
        qkv_grad,
        qv_bias_grad,
        out_grad,
        bias_sums[6],
        up_grad,
        up_bias_grad,
        down_grad,
        bias_sums[7],
    )


def solution(mesh):
    in_specs = (
        P(("dp", "col"), "row"),
        P("dp"),
        P("dp"),
        P(("dp", "col"), "row"),
        P(None, "col"),
        P("col", None, "row"),
        P(None, "row"),
        P("row", None, "col"),
        P(None, "col"),
        P("col", "row"),
        P("row"),
        P("row", "col"),
        P("col"),
        P("col", "row"),
        P("row"),
    )
    out_specs = (
        P(("dp", "col"), "row"),
        P(("dp", "col"), "row"),
        P(None, "col"),
        P("col", None, "row"),
        P(None, "row"),
        P("row", None, "col"),
        P(None, "col"),
        P("col", "row"),
        P("row"),
        P("row", "col"),
        P("col"),
        P("col", "row"),
        P("row"),
    )

    return jax.shard_map(shards, mesh=mesh, in_specs=in_specs, out_specs=out_specs, check_vma=False)
```

```python
from functools import partial
import math

import jax
import jax.numpy as jnp
from jax import lax
from jax.experimental import pallas as pl
from jax.experimental.layout import Layout, with_layout_constraint
from jax.experimental.pallas import tpu as pltpu
from jax.sharding import PartitionSpec as P


HD = 72
norm_epsilon = 1e-06
fast_mode = lax.Precision.HIGH


def contract(left, right, left_dim, right_dim, precision=fast_mode):
    return lax.dot_general(
        left,
        right,
        (((left_dim,), (right_dim,)), ((), ())),
        precision=precision,
        preferred_element_type=jnp.float32,
    )


def row_major(values):
    return with_layout_constraint(values, Layout(major_to_minor=tuple(range(values.ndim))))


def shift_row(values, step):
    count = lax.axis_size("row")
    if step % count == 0:
        return values
    return lax.ppermute(values, "row", [(i, (i + step) % count) for i in range(count)])


def shift_chip(values, step):
    count = lax.axis_size("col") // 2
    if step % count == 0:
        return values
    pairs = [
        (2 * i + core, 2 * ((i + step) % count) + core) for i in range(count) for core in range(2)
    ]
    return lax.ppermute(values, "col", pairs)


def swap_core(values):
    return lax.ppermute(values, "col", [(i, i ^ 1) for i in range(lax.axis_size("col"))])


def swap_dp(values):
    return lax.ppermute(values, "dp", [(0, 1), (1, 0)])


def butterfly(values, axis):
    count = lax.axis_size(axis)
    step = 1
    while step < count:
        values = values + lax.ppermute(values, axis, [(i, i ^ step) for i in range(count)])
        step *= 2
    return values


def row_order():
    count = lax.axis_size("row")
    return sorted(range(count), key=lambda step: (min(step, count - step), step))


def spread(block, ready_chip=(), ready_core=()):
    count = lax.axis_size("row")
    chips = lax.axis_size("col") // 2
    by_step = {0: block}
    own_chips = [shift_chip(block, chip) for chip in range(chips)]
    last = row_order()[-1]
    for step in row_order()[1:-1]:
        if step <= count // 2:
            by_step[step] = shift_row(by_step[step - 1], 1)
        else:
            by_step[step] = shift_row(by_step[(step + 1) % count], -1)
    far = shift_row(by_step[last - 1], 1)
    by_step, ready_chip = lax.optimization_barrier((by_step, ready_chip))
    groups = [own_chips]
    for step in row_order()[1:-1]:
        groups.append([shift_chip(by_step[step], chip) for chip in range(chips)])
    far = jnp.concatenate([shift_chip(far, chip) for chip in range(chips)], axis=0)
    near = jnp.concatenate(sum(groups, []), axis=0)
    near, ready_core = lax.optimization_barrier((near, ready_core))
    return [near, far, swap_core(near), swap_core(far)], ready_chip, ready_core


def by_piece(function, pieces):
    return jnp.concatenate([function(piece) for piece in pieces], axis=0)


def scatter_tokens(partial_rows, tokens, fill, fill_row=lambda earlier, value: value):
    count = lax.axis_size("row")
    chips = lax.axis_size("col") // 2
    half = tokens // 2
    group = half // count
    size = group // chips
    split = half - group
    far = swap_core(partial_rows(half + split, group))
    near = swap_core(partial_rows(half, split))
    far = partial_rows(split, group) + far
    near = partial_rows(0, split) + near
    filled = fill(near)
    sums = {}
    for place, step in reversed(list(enumerate(row_order()))):
        part = far if place == count - 1 else near[place * group : (place + 1) * group]
        total = part[:size]
        for chip in range(1, chips):
            total = total + shift_chip(part[chip * size : (chip + 1) * size], -chip)
        sums[step] = total
    filled = fill_row(sums[1], filled)
    for step in reversed(row_order()[1:]):
        if step <= count // 2:
            sums[step - 1] = sums[step - 1] + shift_row(sums[step], -1)
        else:
            back = (step + 1) % count
            sums[back] = sums[back] + shift_row(sums[step], 1)
    return sums[0], filled


def after(values, earlier):
    return lax.optimization_barrier((values, earlier))[0]


def copy_blocks(size, places_ref, source_ref, target_ref):
    def body(block, carry):
        start = pl.multiple_of(places_ref[block] * size, 8)
        target = pl.multiple_of(block * size, 8)
        target_ref[pl.ds(target, size), :] = source_ref[pl.ds(start, size), :]
        return carry

    lax.fori_loop(0, places_ref.shape[0], body, 0)


def take_blocks(values, places):
    size = values.shape[0] // places.shape[0]
    return pl.pallas_call(
        partial(copy_blocks, size),
        in_specs=[
            pl.BlockSpec(memory_space=pltpu.SMEM),
            pl.BlockSpec(memory_space=pltpu.VMEM),
        ],
        out_specs=pl.BlockSpec(memory_space=pltpu.VMEM),
        out_shape=jax.ShapeDtypeStruct(values.shape, values.dtype),
        cost_estimate=pl.CostEstimate(flops=0, transcendentals=0, bytes_accessed=8 * values.size),
        name="take_blocks",
    )(places, values)


def block_places():
    rows, cols = lax.axis_size("row"), lax.axis_size("col")
    chips = cols // 2
    me_row, me_col = lax.axis_index("row"), lax.axis_index("col")
    tokens_mesh = []
    for core in range(2):
        for step in row_order():
            for chip in range(chips):
                col = (me_col // 2 - chip) % chips * 2 + (me_col % 2 + core) % 2
                tokens_mesh.append(col * rows + (me_row - step) % rows)
    tokens_mesh = jnp.stack(tokens_mesh).astype(jnp.int32)
    numbers = jnp.arange(rows * cols, dtype=jnp.int32)
    mesh_tokens = jnp.sum(
        jnp.where(tokens_mesh[None, :] == numbers[:, None], numbers[None, :], 0), axis=1
    )
    return tokens_mesh, mesh_tokens


def gather_mesh(local):
    return lax.all_gather(local, ("col", "row"), axis=0, tiled=True)


def scatter_mesh(partial_sums):
    return lax.psum_scatter(partial_sums, ("col", "row"), scatter_dimension=0, tiled=True)


def row_outgoing(blocks):
    count = lax.axis_size("row")
    me = lax.axis_index("row")
    return [
        lax.dynamic_index_in_dim(blocks, (me + step) % count, 0, keepdims=False)
        for step in range(count)
    ]


def row_send(outgoing):
    return [shift_row(block, step) for step, block in enumerate(outgoing)]


def row_parts(blocks):
    return row_send(row_outgoing(blocks))


def by_source(parts):
    count = lax.axis_size("row")
    me = lax.axis_index("row")
    stacked = jnp.stack(parts)
    return [
        lax.dynamic_index_in_dim(stacked, (me - row) % count, 0, keepdims=False)
        for row in range(count)
    ]


def move_rows(blocks):
    return row_major(jnp.stack(row_parts(row_major(blocks))))


def own_half(blocks, axis):
    if lax.axis_size("dp") != 2:
        return blocks
    half = blocks.shape[axis] // 2
    return lax.dynamic_slice_in_dim(blocks, lax.axis_index("dp") * half, half, axis)


def share_blocks(mine):
    if lax.axis_size("dp") != 2:
        return mine[None]
    return jnp.stack([mine, swap_dp(mine)])


def order_blocks(both):
    if lax.axis_size("dp") != 2:
        return by_source(list(both[0]))
    me = lax.axis_index("dp")
    low = by_source(list(lax.dynamic_index_in_dim(both, me, 0, keepdims=False)))
    high = by_source(list(lax.dynamic_index_in_dim(both, 1 - me, 0, keepdims=False)))
    return [jnp.concatenate(pair, axis=0) for pair in zip(low, high)]


def pair_halves(grad):
    count = lax.axis_size("row")
    rows = grad.shape[0] // count
    if lax.axis_size("dp") != 2:
        total = grad.reshape(count, rows, grad.shape[1])
        return jnp.zeros_like(total), total
    me = lax.axis_index("dp")
    halves = row_major(grad.reshape(count, 2, rows // 2, grad.shape[1]))
    given = lax.dynamic_index_in_dim(halves, 1 - me, 1, keepdims=False)
    kept = lax.dynamic_index_in_dim(halves, me, 1, keepdims=False)
    return row_major(kept), row_major(given)


def pair_swap(given):
    return swap_dp(given) if lax.axis_size("dp") == 2 else lax.psum(given, "dp")


def dp_stack(values):
    if lax.axis_size("dp") == 2:
        both = jnp.stack([values, swap_dp(values)])
        me = lax.axis_index("dp")
        return jnp.stack(
            [
                lax.dynamic_index_in_dim(both, me, 0, keepdims=False),
                lax.dynamic_index_in_dim(both, 1 - me, 0, keepdims=False),
            ]
        )
    return lax.all_gather(values, "dp", axis=0, tiled=False)


def normalize(values):
    center = jnp.mean(values, axis=1, keepdims=True)
    centred = values - center
    spread_of = jnp.mean(centred * centred, axis=1, keepdims=True)
    inverse = lax.rsqrt(spread_of + norm_epsilon)
    return (centred * inverse, inverse)


def normalize_back(grad_values, normed, inverse):
    totals = jnp.mean(grad_values, axis=1, keepdims=True)
    along = jnp.mean(grad_values * normed, axis=1, keepdims=True)
    return inverse * (grad_values - totals - normed * along)


def shards(
    block_in,
    labels,
    steps_t,
    out_cot,
    class_table,
    w_ada,
    b_ada,
    w_qkv,
    b_qv,
    w_out,
    b_out,
    w_up,
    b_up,
    w_down,
    b_down,
):
    rows = lax.axis_size("row")
    me_row = lax.axis_index("row")
    me_col = lax.axis_index("col")
    tok_local, width_row = block_in.shape
    width = width_row * rows
    width_col = w_out.shape[0]
    heads_col = width_col // HD
    heads_own = max(1, heads_col // rows)
    copies = max(1, rows // heads_col)
    head_width = heads_own * HD
    head_groups = rows // copies
    units_own = w_up.shape[1] // rows

    tokens_mesh, mesh_tokens = block_places()
    tokens = tok_local * lax.axis_size("col")

    feature = me_col * width_col + jnp.arange(width_col)
    half_width = width // 2
    frequency = jnp.exp(
        -math.log(10000.0) * (feature % half_width).astype(jnp.float32) / half_width
    )
    angles = steps_t.astype(jnp.float32)[:, None] * frequency[None, :]
    own_class = lax.dynamic_slice_in_dim(class_table, labels[0], 1, 0)
    condition = own_class + jnp.where(
        feature[None, :] < half_width, jnp.cos(angles), jnp.sin(angles)
    )
    silu_cond, silu_pull = jax.vjp(jax.nn.silu, condition)
    both_own = row_parts(
        jnp.concatenate([block_in, out_cot], axis=1).reshape(
            rows, tok_local // rows, 2 * width_row
        )
    )
    both_own = by_source(both_own)
    in_own = jnp.concatenate([part[:, :width_row] for part in both_own], axis=1)
    cot_own = jnp.concatenate([part[:, width_row:] for part in both_own], axis=1)
    normed_one, inverse_one = normalize(in_own)
    silu_now, qkv_now, out_now, up_now, down_now = after(
        (silu_cond, w_qkv, w_out, w_up, w_down), normed_one
    )
    ada_terms = jnp.sum(silu_now[0][:, None, None] * w_ada, axis=0)

    qkv_blocks = (
        qkv_now.reshape(width_row, 3, head_groups, head_width)
        .transpose(2, 0, 1, 3)
        .reshape(head_groups, width_row, 3 * head_width)
    )
    out_blocks = out_now.reshape(head_groups, head_width, width_row).transpose(0, 2, 1)
    head_blocks = jnp.concatenate([qkv_blocks, out_blocks], axis=2)
    head_blocks = own_half(jnp.repeat(head_blocks, copies, axis=0), 1)
    mlp_blocks = own_half(
        jnp.stack(
            [
                jnp.concatenate(
                    [
                        up_now[:, i * units_own : (i + 1) * units_own],
                        down_now[i * units_own : (i + 1) * units_own].T,
                    ],
                    axis=1,
                )
                for i in range(rows)
            ]
        ),
        1,
    )
    mlp_sent = row_outgoing(mlp_blocks)
    in_pieces, _, mlp_sent = spread(normed_one, (), mlp_sent)
    ada_terms = butterfly(ada_terms, "col") + b_ada
    head_blocks = move_rows(head_blocks)
    mlp_blocks = row_major(jnp.stack(row_send(mlp_sent)))
    small = jnp.concatenate([ada_terms, b_out[None], b_down[None]], axis=0)
    small = [shift_row(small, step) for step in range(rows)]
    small = by_source(after(small, in_pieces[1]))
    small = jnp.concatenate(small, axis=1)[:, None, :]
    shift_one, scale_one, gate_one, shift_two, scale_two, gate_two, out_bias, down_bias = small

    head_blocks = share_blocks(head_blocks)
    head_matrix = jnp.concatenate(order_blocks(after(head_blocks, in_pieces[1])), axis=0)
    qkv_matrix = head_matrix[:, : 3 * head_width]
    out_flip = head_matrix[:, 3 * head_width :]
    hidden_one = [piece * (1.0 + scale_one) + shift_one for piece in in_pieces]
    head_start = (me_row // copies) * head_width
    head_bias = lax.dynamic_slice_in_dim(b_qv, head_start, head_width, 1)
    qkv = by_piece(lambda piece: contract(piece, qkv_matrix, 1, 0), hidden_one)
    qkv = qkv.reshape(tokens, 3, heads_own, HD)
    queries = qkv[:, 0] + head_bias[0].reshape(heads_own, HD)
    keys = qkv[:, 1]
    values = qkv[:, 2] + head_bias[1].reshape(heads_own, HD)
    factor = 1.0 / math.sqrt(HD)
    scores = jnp.einsum("qhd,khd->hqk", queries, keys, precision=fast_mode) * factor
    weights = jnp.exp(scores)
    weights = weights / jnp.sum(weights, axis=2, keepdims=True)
    attended = jnp.einsum("hqk,khd->qhd", weights, values, precision=fast_mode)
    attended = attended.reshape(tokens, head_width)

    def share_mlp(earlier):
        return share_blocks(after(mlp_blocks, earlier))

    attn_out, mlp_blocks = scatter_tokens(
        lambda start, size: contract(attended[start : start + size], out_flip, 1, 1)
        * (1.0 / copies),
        tokens,
        share_mlp,
    )
    attn_out = attn_out + out_bias
    mixed = in_own + gate_one * attn_out
    normed_two, inverse_two = normalize(mixed)
    hidden_two_own = normed_two * (1.0 + scale_two) + shift_two
    mlp_matrix = row_major(
        jnp.concatenate(order_blocks(after(mlp_blocks, hidden_two_own)), axis=0)
    )
    up_matrix = mlp_matrix[:, :units_own]
    down_matrix = mlp_matrix[:, units_own:]

    d_mlp_own = cot_own * gate_two
    cot_all = gather_mesh(after(cot_own, in_pieces[1]))
    d_activated = contract(cot_all, gate_two.reshape(width, 1) * down_matrix, 1, 0)
    d_activated = take_blocks(d_activated, tokens_mesh)
    hidden_two, (up_matrix, down_matrix, d_activated), _ = spread(
        hidden_two_own, (up_matrix, down_matrix, d_activated)
    )
    up_bias = lax.dynamic_slice_in_dim(b_up, me_row * units_own, units_own, 0)
    up_values = by_piece(lambda piece: contract(piece, up_matrix, 1, 0), hidden_two) + up_bias
    activated, gelu_pull = jax.vjp(partial(jax.nn.gelu, approximate=True), up_values)
    (d_up,) = gelu_pull(d_activated)

    def mlp_rest(earlier):
        activated_mesh = take_blocks(after(activated, earlier), mesh_tokens)
        return activated_mesh, contract(activated_mesh, down_matrix, 1, 1)

    d_hidden_two, (activated_mesh, mlp_part) = scatter_tokens(
        lambda start, size: contract(d_up[start : start + size], up_matrix, 1, 1), tokens, mlp_rest
    )

    d_mixed = cot_own + normalize_back(d_hidden_two * (1.0 + scale_two), normed_two, inverse_two)
    d_attn_own = d_mixed * gate_one
    units = after((hidden_two, d_up, cot_all, activated_mesh), d_attn_own)
    up_grad = contract(jnp.concatenate(units[0]), units[1], 0, 0)
    down_grad = contract(units[2], units[3], 0, 0) * gate_two.reshape(width, 1)
    mlp_halves = pair_halves(jnp.concatenate([up_grad, down_grad], axis=1))
    d_attn, mlp_part, (mlp_kept, mlp_given) = spread(d_attn_own, mlp_part, mlp_halves)
    mlp_own = scatter_mesh(mlp_part)
    mlp_given = pair_swap(mlp_given)
    d_attended = by_piece(lambda piece: contract(piece, out_flip, 1, 0), d_attn)
    d_attended = d_attended.reshape(tokens, heads_own, HD)
    d_weights = jnp.einsum("qhd,khd->hqk", d_attended, values, precision=fast_mode)
    row_dots = jnp.sum(weights * d_weights, axis=2, keepdims=True)
    d_scores = weights * (d_weights - row_dots) * factor
    d_query = jnp.einsum("hqk,khd->qhd", d_scores, keys, precision=fast_mode)
    d_key = jnp.einsum("hqk,qhd->khd", d_scores, queries, precision=fast_mode)
    d_value = jnp.einsum("hqk,qhd->khd", weights, d_attended, precision=fast_mode)
    d_qkv = jnp.stack([d_query, d_key, d_value], axis=1).reshape(tokens, 3 * head_width)

    mlp_kept, mlp_given = after((mlp_kept, mlp_given), d_qkv)
    mlp_sent = row_outgoing(row_major(mlp_kept + mlp_given))

    def head_rest(earlier):
        mlp_moved = row_major(jnp.stack(row_send(after(mlp_sent, earlier))))
        d_heads = after(d_qkv, earlier)
        qkv_grad = contract(jnp.concatenate(hidden_one), d_heads, 0, 0)
        out_grad = contract(jnp.concatenate(d_attn), after(attended, earlier), 0, 0)
        kept, given = pair_halves(jnp.concatenate([qkv_grad, out_grad], axis=1))
        given = pair_swap(given)
        return mlp_moved, kept, given

    def head_rest_row(earlier, filled):
        mlp_moved, kept, given = filled
        mlp_shared = share_blocks(after(mlp_moved, earlier))
        return mlp_shared, move_rows(after(kept + given, earlier))

    d_hidden_one, (mlp_shared, head_moved) = scatter_tokens(
        lambda start, size: contract(d_qkv[start : start + size], qkv_matrix, 1, 1)
        * (1.0 / copies),
        tokens,
        head_rest,
        head_rest_row,
    )
    mlp_own = after(mlp_own, d_hidden_one) + down_bias
    in_grad = d_mixed + normalize_back(
        d_hidden_one * (1.0 + scale_one), normed_one, inverse_one
    )
    block_out = mixed + gate_two * mlp_own
    results = jnp.stack(
        [
            jnp.concatenate(
                [
                    block_out[:, i * width_row : (i + 1) * width_row],
                    in_grad[:, i * width_row : (i + 1) * width_row],
                ],
                axis=1,
            )
            for i in range(rows)
        ]
    )

    unit_sums = jnp.concatenate([jnp.sum(d_up, axis=0), jnp.sum(d_qkv, axis=0)])
    unit_sums = jnp.stack(by_source([shift_row(unit_sums, step) for step in range(rows)]))
    own_sums = jnp.stack(
        [
            jnp.sum(d_hidden_one, axis=0),
            jnp.sum(d_hidden_one * normed_one, axis=0),
            jnp.sum(d_mixed * attn_out, axis=0),
            jnp.sum(d_hidden_two, axis=0),
            jnp.sum(d_hidden_two * normed_two, axis=0),
            jnp.sum(cot_own * mlp_own, axis=0),
            jnp.sum(d_attn_own, axis=0),
            jnp.sum(d_mlp_own, axis=0),
        ]
    )
    results = row_parts(results)
    own_sums = butterfly(own_sums, "col")
    own_sums = butterfly(own_sums, "row")
    head_grad = share_blocks(after(head_moved, d_hidden_one))
    head_grad = order_blocks(after(head_grad, own_sums))[::copies]
    qkv_grad = jnp.stack(
        [part[:, : 3 * head_width].reshape(width_row, 3, head_width) for part in head_grad],
        axis=2,
    ).reshape(width_row, 3, width_col)
    out_grad = jnp.concatenate([part[:, 3 * head_width :].T for part in head_grad], axis=0)
    mlp_grad = order_blocks(after(mlp_shared, own_sums))
    up_grad = jnp.concatenate([part[:, :units_own] for part in mlp_grad], axis=1)
    down_grad = jnp.concatenate([part[:, units_own:].T for part in mlp_grad], axis=0)
    own_sums = lax.dynamic_slice_in_dim(own_sums, me_row * width_row, width_row, 1)
    label_row = jnp.broadcast_to(labels.astype(jnp.float32), (128,))
    unit_size = unit_sums.size
    pack = dp_stack(
        jnp.concatenate([unit_sums.reshape(-1), own_sums.reshape(-1), silu_cond[0], label_row])
    )
    unit_sums = jnp.sum(pack[:, :unit_size], axis=0).reshape(rows, -1)
    up_bias_grad = unit_sums[:, :units_own].reshape(-1)
    qkv_sums = unit_sums[::copies, units_own:].reshape(head_groups, 3, head_width)
    qv_bias_grad = jnp.stack([qkv_sums[:, 0].reshape(-1), qkv_sums[:, 2].reshape(-1)])
    sums_all = pack[:, unit_size : unit_size + 8 * width_row].reshape(-1, 8, width_row)
    silu_all = pack[:, unit_size + 8 * width_row : -128]
    bias_sums = jnp.sum(sums_all, axis=0)
    ada_grad = jnp.sum(silu_all[:, :, None, None] * sums_all[:, None, :6], axis=0)
    silu_grads = jnp.sum(own_sums[None, :6] * w_ada, axis=(1, 2))[None]
    silu_grads = butterfly(silu_grads, "row")
    (cond_grad,) = silu_pull(silu_grads)
    cond_all = dp_stack(cond_grad[0])
    results = jnp.concatenate(by_source(after(results, cond_all)), axis=0)
    label_all = pack[:, -1].astype(jnp.int32)
    classes = jnp.arange(class_table.shape[0])
    table_grad = jnp.sum(
        jnp.where(
            label_all[:, None, None] == classes[None, :, None], cond_all[:, None, :], 0.0
        ),
        axis=0,
    )
    return (
        results[:, :width_row],
        results[:, width_row:],
        table_grad,
        ada_grad,
        bias_sums[:6],
        qkv_grad,
        qv_bias_grad,
        out_grad,
        bias_sums[6],
        up_grad,
        up_bias_grad,
        down_grad,
        bias_sums[7],
    )


def solution(mesh):
    in_specs = (
        P(("dp", "col"), "row"),
        P("dp"),
        P("dp"),
        P(("dp", "col"), "row"),
        P(None, "col"),
        P("col", None, "row"),
        P(None, "row"),
        P("row", None, "col"),
        P(None, "col"),
        P("col", "row"),
        P("row"),
        P("row", "col"),
        P("col"),
        P("col", "row"),
        P("row"),
    )
    out_specs = (
        P(("dp", "col"), "row"),
        P(("dp", "col"), "row"),
        P(None, "col"),
        P("col", None, "row"),
        P(None, "row"),
        P("row", None, "col"),
        P(None, "col"),
        P("col", "row"),
        P("row"),
        P("row", "col"),
        P("col"),
        P("col", "row"),
        P("row"),
    )

    return jax.shard_map(shards, mesh=mesh, in_specs=in_specs, out_specs=out_specs, check_vma=False)
```
